32 devices in a mesh: groups: 2 (over y), context: 8 (over z, x), tensor: 2 (over core).
Axes of the slice: x: 2, y: 2, z: 4, core: 2. Of those that a mesh axis runs over, the one named last changes fastest.
Arguments:
- query_rows: bfloat16 [8192, 2048], P(('groups', 'context'), 'tensor'), parts along dimension 0, may hold values from -16 to 16, as said below
- key_rows: bfloat16 [8192, 2048], P(('groups', 'context'), 'tensor'), parts along dimension 0, may hold values from -6 to 6, as said below
- value_rows: bfloat16 [8192, 2048], P(('groups', 'context'), 'tensor'), parts along dimension 0, may hold values from -6 to 6
- selection: int32 [16, 16], P('tensor', ('groups', 'context')), parts along dimension 1, may hold values from 0 to 7, as said below
Outputs:
- attended: bfloat16 [8192, 2048], P(('groups', 'context'), 'tensor'), parts along dimension 0
- sort_logits: float32 [16, 16, 8], P('tensor', ('groups', 'context')), parts along dimension 1
The draws below stay inside these ranges and needn't reach their ends.
There are 2 independent parts, one for each index of `groups`. The reference program is written for one: setup_inputs(seed, part) draws one part's arguments, and reference() takes and returns one part's arrays. A program takes and returns all parts, laid end to end along the dimension named above; each array names one. Nothing has to cross between parts.
Inputs may be any that keep to these rules, and one draw needn't show every extreme that they name: `query_rows`: Queries; of order a few units. `key_rows`: Keys; of order one. `selection`: for each head, a permutation of the 8 blocks.
All inputs are finite; a program needn't handle non-finite values.
Results may differ from the reference program's by a relative error of at most 0.0048.
Values may be sent and summed in bfloat16 or wider, within the bound.
No kernel may reach another device: no remote copies, remote signals or barrier semaphores. Data moves between devices by JAX's collectives and lax.ppermute only.
A program may use at most 64 MiB of HBM per device.

```python
import math
import jax
import jax.numpy as jnp
from jax import lax

H = 16
DH = 128
BS = 512
NB = 8
TOKENS = 4096


def draw_query_rows(key, part):
    base = jnp.clip(jax.random.normal(jax.random.fold_in(key, 3), (TOKENS, H * DH), jnp.float32), -6.0, 6.0)
    result = 2.5 * base
    return result.astype(jnp.bfloat16)


def draw_key_rows(key, part):
    result = jnp.clip(jax.random.normal(jax.random.fold_in(key, 4), (TOKENS, H * DH), jnp.float32), -6.0, 6.0)
    return result.astype(jnp.bfloat16)


def draw_selection(key, part):
    head_keys = jax.random.split(jax.random.fold_in(key, 29), H)
    return jax.vmap(lambda one_key: jax.random.permutation(one_key, NB))(head_keys).astype(jnp.int32)


def level_of(stream_key, dims, cuts, low, largest):
    level = 1.0
    for dim, blocks in cuts:
        heights = jax.random.uniform(jax.random.fold_in(jax.random.fold_in(stream_key, 6), dim), (blocks,), jnp.float32, low / len(cuts), largest / len(cuts))
        level = level * jnp.repeat(jnp.exp(heights), dims[dim] // blocks).reshape((-1,) + (1,) * (len(dims) - 1 - dim))
    return level


def scatter_about(rng, extent, deviation, most, cuts=(), held_as=jnp.bfloat16):
    entries = jax.random.normal(rng, extent, jnp.float32) * deviation
    if len(cuts) > 0:
        entries = level_of(rng, extent, cuts, -0.22, 0.18) * entries
    return jnp.clip(entries, min=-most, max=most).astype(held_as)


def setup_inputs(seed: int = 0, part: int = 0) -> dict:
    key_list = jax.random.split(jax.random.key(seed), 5)
    part_splits = jax.random.split(jax.random.fold_in(key_list[4], part), 5)
    query_rows = draw_query_rows(jax.random.fold_in(jax.random.fold_in(key_list[4], part), 71), part)
    key_rows = draw_key_rows(jax.random.fold_in(jax.random.fold_in(key_list[4], part), 71), part)
    value_rows = scatter_about(part_splits[2], (TOKENS, H * DH), 1.0, 6.0, ((0, 8), (1, 2)))
    selection = draw_selection(jax.random.fold_in(jax.random.fold_in(key_list[4], part), 71), part)
    return {"query_rows": query_rows, "key_rows": key_rows, "value_rows": value_rows, "selection": selection}


def block_partial(query_block, key_block, value_block):
    scores = jnp.dot(query_block, key_block.T, preferred_element_type=jnp.float32) * (1.0 / math.sqrt(DH))
    row_max = lax.optimization_barrier(jnp.max(scores, axis=1, keepdims=True))
    weights = jnp.exp(scores - row_max).astype(jnp.bfloat16)
    row_total = lax.optimization_barrier(jnp.sum(weights.astype(jnp.float32), axis=1, keepdims=True))
    partial_sum = jnp.dot(weights, value_block, preferred_element_type=jnp.float32)
    return (row_max, row_total, partial_sum)

def combine_parts(own_part, far_part):
    own_max, own_total, own_sum = own_part
    far_max, far_total, far_sum = far_part
    joint = jnp.maximum(own_max, far_max)
    own_factor = jnp.exp(own_max - joint)
    far_factor = jnp.exp(far_max - joint)
    merged = (own_factor * own_sum + far_factor * far_sum) / (own_factor * own_total + far_factor * far_total)
    return merged.astype(jnp.bfloat16)

def pooled(rows_in):
    sums = lax.optimization_barrier(jnp.sum(rows_in.reshape(NB, BS, H * DH), axis=1, dtype=jnp.float32)) / math.sqrt(BS)
    return sums.astype(jnp.bfloat16).reshape(NB, H, DH)

def reference(query_rows, key_rows, value_rows, selection):
    pooled_q = pooled(query_rows)
    pooled_k = pooled(key_rows)
    sort_logits = jnp.einsum('bhd,chd->hbc', pooled_q.astype(jnp.float32), pooled_k.astype(jnp.float32)) / math.sqrt(DH)
    query_grid = query_rows.reshape(NB, BS, H, DH)
    key_grid = key_rows.reshape(NB, BS, H, DH)
    value_grid = value_rows.reshape(NB, BS, H, DH)
    zero_index = jnp.zeros((), jnp.int32)

    def one_pair(pair_index):
        head = (pair_index // NB).astype(jnp.int32)
        block = (pair_index % NB).astype(jnp.int32)
        source = selection[head, block].astype(jnp.int32)

        def take(array, which):
            return lax.dynamic_slice(array, (which, zero_index, head, zero_index), (1, BS, 1, DH)).reshape(BS, DH)
        query_block = take(query_grid, block)
        own = block_partial(query_block, take(key_grid, block), take(value_grid, block))
        far = block_partial(query_block, take(key_grid, source), take(value_grid, source))
        return combine_parts(own, far)
    outputs = lax.map(one_pair, jnp.arange(H * NB, dtype=jnp.int32))
    attended = outputs.reshape(H, NB, BS, DH).transpose(1, 2, 0, 3).reshape(NB * BS, H * DH)
    return (attended, sort_logits)
```

```python
import functools
import math

import jax
import jax.numpy as jnp
from jax import lax
from jax.experimental import pallas as pl
from jax.experimental.pallas import tpu as pltpu
from jax.sharding import PartitionSpec as P

DH = 128
BS = 512
BF16 = jnp.bfloat16
F32 = jnp.float32


def block_partial(query_block, key_block, value_block):
    scores = jnp.dot(query_block, key_block.T, preferred_element_type=jnp.float32) * (
        1.0 / math.sqrt(DH)
    )
    row_max = jnp.max(scores, axis=1, keepdims=True)
    weights = jnp.exp(scores - row_max).astype(jnp.bfloat16)
    row_total = jnp.sum(weights.astype(jnp.float32), axis=1, keepdims=True)
    partial_sum = jnp.dot(weights, value_block, preferred_element_type=jnp.float32)
    return (row_max, row_total, partial_sum)


def combine_parts(own_part, far_part):
    own_max, own_total, own_sum = own_part
    far_max, far_total, far_sum = far_part
    joint = jnp.maximum(own_max, far_max)
    own_factor = jnp.exp(own_max - joint)
    far_factor = jnp.exp(far_max - joint)
    merged = (own_factor * own_sum + far_factor * far_sum) / (
        own_factor * own_total + far_factor * far_total
    )
    return merged.astype(jnp.bfloat16)


def any_size(query_rows, key_rows, value_rows, selection):
    members = lax.axis_size("context")
    tok_rows, width = query_rows.shape
    blocks = tok_rows // BS
    head_count = width // DH
    piece_rows = BS // members

    def pooled(rows_in):
        sums = jnp.sum(rows_in.reshape(blocks, BS, width), axis=1, dtype=jnp.float32) / math.sqrt(
            BS
        )
        return sums.astype(jnp.bfloat16).reshape(blocks, head_count, DH).transpose(1, 0, 2)

    pooled_q = pooled(query_rows)
    pooled_k = pooled(key_rows)
    products = jnp.einsum(
        "hbd,hcd->hbc",
        pooled_q,
        lax.all_gather(pooled_k, "context", axis=1, tiled=True),
        preferred_element_type=jnp.float32,
    )
    sort_logits = products / math.sqrt(DH)
    wanted = lax.all_gather(selection, "context", axis=1, tiled=True)
    query_grid = query_rows.reshape(blocks, BS, head_count, DH)
    key_grid = key_rows.reshape(blocks, BS, head_count, DH)
    value_grid = value_rows.reshape(blocks, BS, head_count, DH)
    pair_ids = jnp.arange(blocks * head_count, dtype=jnp.int32)

    def slice_pair(array, block, head):
        return lax.dynamic_slice(array, (block, 0, head, 0), (1, BS, 1, DH)).reshape(BS, DH)

    def pick_rows(held, table):
        inner = held.shape[-1] // head_count
        order_ids = table.reshape(head_count, members, blocks).transpose(2, 1, 0)
        source_dev = (order_ids // blocks)[:, :, None, :]
        source_blk = (order_ids % blocks)[:, :, None, :]
        row_ids = jnp.arange(piece_rows)[None, None, :, None]
        head_ids = jnp.arange(head_count)[None, None, None, :]
        grid = held.reshape(blocks, members, piece_rows, head_count, inner)
        return grid[source_blk, source_dev, row_ids, head_ids].reshape(
            blocks, members, piece_rows, head_count * inner
        )

    spread_k = key_rows.reshape(blocks, members, piece_rows, width)
    spread_v = value_rows.reshape(blocks, members, piece_rows, width)
    held_k = lax.all_to_all(spread_k, "context", split_axis=1, concat_axis=1, tiled=True)
    held_v = lax.all_to_all(spread_v, "context", split_axis=1, concat_axis=1, tiled=True)
    far_k = lax.all_to_all(
        pick_rows(held_k, wanted), "context", split_axis=1, concat_axis=1, tiled=True
    )
    far_v = lax.all_to_all(
        pick_rows(held_v, wanted), "context", split_axis=1, concat_axis=1, tiled=True
    )
    far_keys = far_k.reshape(blocks, BS, head_count, DH)
    far_values = far_v.reshape(blocks, BS, head_count, DH)

    def both_pair(pair_index):
        block = pair_index // head_count
        head = pair_index % head_count
        query_block = slice_pair(query_grid, block, head)
        own = block_partial(
            query_block, slice_pair(key_grid, block, head), slice_pair(value_grid, block, head)
        )
        far = block_partial(
            query_block, slice_pair(far_keys, block, head), slice_pair(far_values, block, head)
        )
        return combine_parts(own, far)

    outputs = lax.map(both_pair, pair_ids)
    attended = (
        outputs.reshape(blocks, head_count, BS, DH).transpose(0, 2, 1, 3).reshape(tok_rows, width)
    )
    return (attended, sort_logits)


def pick_kernel(members, heads, table, *refs):
    pieces, outs, held = refs[:members], refs[members : 2 * members], refs[2 * members]
    for e in range(members):
        held[e] = pieces[e][...]
    for d in range(members):
        for h in range(heads):
            cols = pl.ds(h * DH, DH)
            outs[d][:, cols] = held[table[d, h], :, cols]


def pick_pieces(table, pieces):
    members = len(pieces)
    rows, width = pieces[0].shape
    spec = pl.BlockSpec((rows, width), lambda i, t: (0, 0))
    return pl.pallas_call(
        functools.partial(pick_kernel, members, width // DH),
        grid_spec=pltpu.PrefetchScalarGridSpec(
            num_scalar_prefetch=1,
            grid=(1,),
            in_specs=[spec] * members,
            out_specs=[spec] * members,
            scratch_shapes=[pltpu.VMEM((members, rows, width), BF16)],
        ),
        out_shape=[jax.ShapeDtypeStruct((rows, width), BF16)] * members,
        cost_estimate=pl.CostEstimate(
            flops=0, transcendentals=0, bytes_accessed=4 * members * rows * width
        ),
    )(table, *pieces)


def scores_kernel(members, q_ref, k_ref, v_ref, *refs):
    far_k, (own_ref, w_ref, kf_ref) = refs[:members], refs[members:]
    rows = far_k[0].shape[0]
    for e in range(members):
        kf_ref[pl.ds(e * rows, rows), :] = far_k[e][...]
    q = q_ref[...]

    def part(keys):
        s = lax.dot_general(
            q, keys, (((1,), (1,)), ((), ())), preferred_element_type=F32
        ) * (1.0 / math.sqrt(DH))
        top = jnp.max(s, axis=1, keepdims=True)
        w = jnp.exp(s - top).astype(BF16)
        return top, w, jnp.sum(w.astype(F32), axis=1, keepdims=True)

    own_max, own_w, own_total = part(k_ref[...])
    own_sum = jnp.dot(own_w, v_ref[...], preferred_element_type=F32)
    far_max, far_w, far_total = part(kf_ref[...])
    joint = jnp.maximum(own_max, far_max)
    own_e = jnp.exp(own_max - joint)
    far_e = jnp.exp(far_max - joint)
    inverse = 1.0 / (own_e * own_total + far_e * far_total)
    own_ref[...] = own_sum * (own_e * inverse)
    w_ref[0] = (far_w.astype(F32) * (far_e * inverse)).astype(BF16)


def score_parts(q, k, v, far_k):
    members = len(far_k)
    tok, width = q.shape
    heads = width // DH
    rows = far_k[0].shape[0]
    whole = pl.BlockSpec((tok, DH), lambda h: (0, h))
    piece = pl.BlockSpec((rows, DH), lambda h: (0, h))
    return pl.pallas_call(
        functools.partial(scores_kernel, members),
        grid=(heads,),
        in_specs=[whole] * 3 + [piece] * members,
        out_specs=[whole, pl.BlockSpec((1, tok, BS), lambda h: (h, 0, 0))],
        out_shape=[
            jax.ShapeDtypeStruct((tok, width), F32),
            jax.ShapeDtypeStruct((heads, tok, BS), BF16),
        ],
        scratch_shapes=[pltpu.VMEM((BS, DH), BF16)],
        compiler_params=pltpu.CompilerParams(vmem_limit_bytes=40 << 20),
        cost_estimate=pl.CostEstimate(
            flops=6 * tok * BS * width,
            transcendentals=2 * heads * tok * BS,
            bytes_accessed=12 * tok * width + 2 * heads * tok * BS,
        ),
    )(q, k, v, *far_k)


def finish_kernel(members, w_ref, own_ref, *refs):
    far_v, (out_ref, vf_ref) = refs[:members], refs[members:]
    rows = far_v[0].shape[0]
    for e in range(members):
        vf_ref[pl.ds(e * rows, rows), :] = far_v[e][...]
    out_ref[...] = (
        own_ref[...] + jnp.dot(w_ref[0], vf_ref[...], preferred_element_type=F32)
    ).astype(BF16)


def finish(w, own, far_v):
    members = len(far_v)
    tok, width = own.shape
    heads = width // DH
    rows = far_v[0].shape[0]
    whole = pl.BlockSpec((tok, DH), lambda h: (0, h))
    piece = pl.BlockSpec((rows, DH), lambda h: (0, h))
    return pl.pallas_call(
        functools.partial(finish_kernel, members),
        grid=(heads,),
        in_specs=[pl.BlockSpec((1, tok, BS), lambda h: (h, 0, 0)), whole] + [piece] * members,
        out_specs=whole,
        out_shape=jax.ShapeDtypeStruct((tok, width), BF16),
        scratch_shapes=[pltpu.VMEM((BS, DH), BF16)],
        compiler_params=pltpu.CompilerParams(vmem_limit_bytes=40 << 20),
        cost_estimate=pl.CostEstimate(
            flops=2 * tok * BS * width,
            transcendentals=0,
            bytes_accessed=8 * tok * width + 2 * heads * tok * BS,
        ),
    )(w, own, *far_v)


def power_of_two(query_rows, key_rows, value_rows, selection):
    members = lax.axis_size("context")
    me = lax.axis_index("context")
    tok, width = query_rows.shape
    heads = width // DH
    rows = BS // members

    def send(x, d):
        return lax.ppermute(x, "context", [(i, i ^ d) for i in range(members)])

    order = sorted(range(1, members), reverse=True)

    def exchange(chunks):
        got = list(chunks)
        for d in order:
            got[d] = send(chunks[d], d)
        return got

    def split(array):
        return [array[d * rows : (d + 1) * rows] for d in range(members)]

    def pooled(array):
        return (jnp.sum(array, axis=0, dtype=F32) / math.sqrt(BS)).astype(BF16)

    chosen = jnp.pad(selection[:, 0].astype(BF16), (0, width - heads))
    shared = jnp.stack([pooled(key_rows), chosen])[None]
    d = 1
    while d < members:
        shared = jnp.concatenate([shared, send(shared, d)], axis=0)
        d *= 2
    table = me ^ shared[:, 1, :heads].astype(jnp.int32)

    held_k = exchange(split(key_rows))
    held_v = exchange(split(value_rows))
    far_k = exchange(pick_pieces(table, held_k))
    far_v = exchange(pick_pieces(table, held_v))

    own, w = score_parts(query_rows, key_rows, value_rows, far_k)
    attended = finish(w, own, far_v)

    pooled_k = shared[:, 0][me ^ jnp.arange(members)]
    sort_logits = jnp.einsum(
        "hd,chd->hc",
        pooled(query_rows).reshape(heads, DH),
        pooled_k.reshape(members, heads, DH),
        preferred_element_type=F32,
    ) / math.sqrt(DH)
    return attended, sort_logits.reshape(heads, 1, members)


def solution(mesh):
    members = mesh.shape["context"]

    def per_device(query_rows, key_rows, value_rows, selection):
        fits = members & (members - 1) == 0 and BS % (16 * members) == 0
        if query_rows.shape[0] == BS and fits:
            return power_of_two(query_rows, key_rows, value_rows, selection)
        return any_size(query_rows, key_rows, value_rows, selection)

    placed = (
        P(("groups", "context"), "tensor"),
        P(("groups", "context"), "tensor"),
        P(("groups", "context"), "tensor"),
        P("tensor", ("groups", "context")),
    )
    return jax.shard_map(
        per_device,
        mesh=mesh,
        in_specs=placed,
        out_specs=(P(("groups", "context"), "tensor"), P("tensor", ("groups", "context"), None)),
        check_vma=False,
    )
```

```python
import functools
import math

import jax
import jax.numpy as jnp
from jax import lax
from jax.experimental import pallas as pl
from jax.experimental.pallas import tpu as pltpu
from jax.sharding import PartitionSpec as P

DH = 128
BS = 512
BF16 = jnp.bfloat16
F32 = jnp.float32


def block_partial(query_block, key_block, value_block):
    scores = jnp.dot(query_block, key_block.T, preferred_element_type=jnp.float32) * (
        1.0 / math.sqrt(DH)
    )
    row_max = jnp.max(scores, axis=1, keepdims=True)
    weights = jnp.exp(scores - row_max).astype(jnp.bfloat16)
    row_total = jnp.sum(weights.astype(jnp.float32), axis=1, keepdims=True)
    partial_sum = jnp.dot(weights, value_block, preferred_element_type=jnp.float32)
    return (row_max, row_total, partial_sum)


def combine_parts(own_part, far_part):
    own_max, own_total, own_sum = own_part
    far_max, far_total, far_sum = far_part
    joint = jnp.maximum(own_max, far_max)
    own_factor = jnp.exp(own_max - joint)
    far_factor = jnp.exp(far_max - joint)
    merged = (own_factor * own_sum + far_factor * far_sum) / (
        own_factor * own_total + far_factor * far_total
    )
    return merged.astype(jnp.bfloat16)


def any_size(query_rows, key_rows, value_rows, selection):
    members = lax.axis_size("context")
    tok_rows, width = query_rows.shape
    blocks = tok_rows // BS
    head_count = width // DH
    piece_rows = BS // members

    def pooled(rows_in):
        sums = jnp.sum(rows_in.reshape(blocks, BS, width), axis=1, dtype=jnp.float32) / math.sqrt(
            BS
        )
        return sums.astype(jnp.bfloat16).reshape(blocks, head_count, DH).transpose(1, 0, 2)

    pooled_q = pooled(query_rows)
    pooled_k = pooled(key_rows)
    products = jnp.einsum(
        "hbd,hcd->hbc",
        pooled_q,
        lax.all_gather(pooled_k, "context", axis=1, tiled=True),
        preferred_element_type=jnp.float32,
    )
    sort_logits = products / math.sqrt(DH)
    wanted = lax.all_gather(selection, "context", axis=1, tiled=True)
    query_grid = query_rows.reshape(blocks, BS, head_count, DH)
    key_grid = key_rows.reshape(blocks, BS, head_count, DH)
    value_grid = value_rows.reshape(blocks, BS, head_count, DH)
    pair_ids = jnp.arange(blocks * head_count, dtype=jnp.int32)

    def slice_pair(array, block, head):
        return lax.dynamic_slice(array, (block, 0, head, 0), (1, BS, 1, DH)).reshape(BS, DH)

    def pick_rows(held, table):
        inner = held.shape[-1] // head_count
        order_ids = table.reshape(head_count, members, blocks).transpose(2, 1, 0)
        source_dev = (order_ids // blocks)[:, :, None, :]
        source_blk = (order_ids % blocks)[:, :, None, :]
        row_ids = jnp.arange(piece_rows)[None, None, :, None]
        head_ids = jnp.arange(head_count)[None, None, None, :]
        grid = held.reshape(blocks, members, piece_rows, head_count, inner)
        return grid[source_blk, source_dev, row_ids, head_ids].reshape(
            blocks, members, piece_rows, head_count * inner
        )

    spread_k = key_rows.reshape(blocks, members, piece_rows, width)
    spread_v = value_rows.reshape(blocks, members, piece_rows, width)
    held_k = lax.all_to_all(spread_k, "context", split_axis=1, concat_axis=1, tiled=True)
    held_v = lax.all_to_all(spread_v, "context", split_axis=1, concat_axis=1, tiled=True)
    far_k = lax.all_to_all(
        pick_rows(held_k, wanted), "context", split_axis=1, concat_axis=1, tiled=True
    )
    far_v = lax.all_to_all(
        pick_rows(held_v, wanted), "context", split_axis=1, concat_axis=1, tiled=True
    )
    far_keys = far_k.reshape(blocks, BS, head_count, DH)
    far_values = far_v.reshape(blocks, BS, head_count, DH)

    def both_pair(pair_index):
        block = pair_index // head_count
        head = pair_index % head_count
        query_block = slice_pair(query_grid, block, head)
        own = block_partial(
            query_block, slice_pair(key_grid, block, head), slice_pair(value_grid, block, head)
        )
        far = block_partial(
            query_block, slice_pair(far_keys, block, head), slice_pair(far_values, block, head)
        )
        return combine_parts(own, far)

    outputs = lax.map(both_pair, pair_ids)
    attended = (
        outputs.reshape(blocks, head_count, BS, DH).transpose(0, 2, 1, 3).reshape(tok_rows, width)
    )
    return (attended, sort_logits)


def pick_kernel(members, heads, me_ref, chosen, *refs):
    pieces, outs, held = refs[:members], refs[members : 2 * members], refs[2 * members]
    me = me_ref[0]
    for e in range(members):
        held[e] = pieces[e][...]
    for d in range(members):
        for h in range(heads):
            cols = pl.ds(h * DH, DH)
            outs[d][:, cols] = held[me ^ chosen[me ^ d, h], :, cols]


def pick_pieces(me, chosen, pieces):
    members = len(pieces)
    rows, width = pieces[0].shape
    spec = pl.BlockSpec((rows, width), lambda i, m, t: (0, 0))
    return pl.pallas_call(
        functools.partial(pick_kernel, members, width // DH),
        grid_spec=pltpu.PrefetchScalarGridSpec(
            num_scalar_prefetch=2,
            grid=(1,),
            in_specs=[spec] * members,
            out_specs=[spec] * members,
            scratch_shapes=[pltpu.VMEM((members, rows, width), BF16)],
        ),
        out_shape=[jax.ShapeDtypeStruct((rows, width), BF16)] * members,
        cost_estimate=pl.CostEstimate(
            flops=0, transcendentals=0, bytes_accessed=4 * members * rows * width
        ),
    )(me, chosen, *pieces)


def softmax_part(q, keys):
    s = lax.dot_general(q, keys, (((1,), (1,)), ((), ())), preferred_element_type=F32) * (
        1.0 / math.sqrt(DH)
    )
    top = jnp.max(s, axis=1, keepdims=True)
    w = jnp.exp(s - top).astype(BF16)
    return top, w, jnp.sum(w.astype(F32), axis=1, keepdims=True)


def own_kernel(q_ref, k_ref, v_ref, sum_ref, top_ref, total_ref):
    top, w, total = softmax_part(q_ref[...], k_ref[...])
    sum_ref[...] = jnp.dot(w, v_ref[...], preferred_element_type=F32)
    top_ref[0] = top
    total_ref[0] = total


def own_part(q, k, v):
    tok, width = q.shape
    heads = width // DH
    whole = pl.BlockSpec((tok, DH), lambda h: (0, h))
    column = pl.BlockSpec((1, tok, 1), lambda h: (h, 0, 0))
    return pl.pallas_call(
        own_kernel,
        grid=(heads,),
        in_specs=[whole] * 3,
        out_specs=[whole, column, column],
        out_shape=[
            jax.ShapeDtypeStruct((tok, width), F32),
            jax.ShapeDtypeStruct((heads, tok, 1), F32),
            jax.ShapeDtypeStruct((heads, tok, 1), F32),
        ],
        compiler_params=pltpu.CompilerParams(vmem_limit_bytes=32 << 20),
        cost_estimate=pl.CostEstimate(
            flops=4 * tok * BS * width,
            transcendentals=heads * tok * BS,
            bytes_accessed=10 * tok * width,
        ),
    )(q, k, v)


def scores_kernel(members, q_ref, sum_ref, top_ref, total_ref, *refs):
    far_k, (own_ref, w_ref, kf_ref) = refs[:members], refs[members:]
    rows = far_k[0].shape[0]
    for e in range(members):
        kf_ref[pl.ds(e * rows, rows), :] = far_k[e][...]
    far_max, far_w, far_total = softmax_part(q_ref[...], kf_ref[...])
    own_max = top_ref[0]
    joint = jnp.maximum(own_max, far_max)
    own_e = jnp.exp(own_max - joint)
    far_e = jnp.exp(far_max - joint)
    inverse = 1.0 / (own_e * total_ref[0] + far_e * far_total)
    own_ref[...] = sum_ref[...] * (own_e * inverse)
    w_ref[0] = (far_w.astype(F32) * (far_e * inverse)).astype(BF16)


def score_parts(q, own, far_k):
    members = len(far_k)
    tok, width = q.shape
    heads = width // DH
    rows = far_k[0].shape[0]
    whole = pl.BlockSpec((tok, DH), lambda h: (0, h))
    column = pl.BlockSpec((1, tok, 1), lambda h: (h, 0, 0))
    piece = pl.BlockSpec((rows, DH), lambda h: (0, h))
    return pl.pallas_call(
        functools.partial(scores_kernel, members),
        grid=(heads,),
        in_specs=[whole, whole, column, column] + [piece] * members,
        out_specs=[whole, pl.BlockSpec((1, tok, BS), lambda h: (h, 0, 0))],
        out_shape=[
            jax.ShapeDtypeStruct((tok, width), F32),
            jax.ShapeDtypeStruct((heads, tok, BS), BF16),
        ],
        scratch_shapes=[pltpu.VMEM((BS, DH), BF16)],
        compiler_params=pltpu.CompilerParams(vmem_limit_bytes=32 << 20),
        cost_estimate=pl.CostEstimate(
            flops=2 * tok * BS * width,
            transcendentals=heads * tok * BS,
            bytes_accessed=12 * tok * width + 2 * heads * tok * BS,
        ),
    )(q, *own, *far_k)


def finish_kernel(members, w_ref, own_ref, *refs):
    far_v, (out_ref, vf_ref) = refs[:members], refs[members:]
    rows = far_v[0].shape[0]
    for e in range(members):
        vf_ref[pl.ds(e * rows, rows), :] = far_v[e][...]
    out_ref[...] = (
        own_ref[...] + jnp.dot(w_ref[0], vf_ref[...], preferred_element_type=F32)
    ).astype(BF16)


def finish(w, own, far_v):
    members = len(far_v)
    tok, width = own.shape
    heads = width // DH
    rows = far_v[0].shape[0]
    whole = pl.BlockSpec((tok, DH), lambda h: (0, h))
    piece = pl.BlockSpec((rows, DH), lambda h: (0, h))
    return pl.pallas_call(
        functools.partial(finish_kernel, members),
        grid=(heads,),
        in_specs=[pl.BlockSpec((1, tok, BS), lambda h: (h, 0, 0)), whole] + [piece] * members,
        out_specs=whole,
        out_shape=jax.ShapeDtypeStruct((tok, width), BF16),
        scratch_shapes=[pltpu.VMEM((BS, DH), BF16)],
        compiler_params=pltpu.CompilerParams(vmem_limit_bytes=32 << 20),
        cost_estimate=pl.CostEstimate(
            flops=2 * tok * BS * width,
            transcendentals=0,
            bytes_accessed=8 * tok * width + 2 * heads * tok * BS,
        ),
    )(w, own, *far_v)


def after(x, *earlier):
    return lax.optimization_barrier((x, *earlier))[0]


IN_FLIGHT = 5


def power_of_two(query_rows, key_rows, value_rows, selection):
    members = lax.axis_size("context")
    me = lax.axis_index("context")
    tok, width = query_rows.shape
    heads = width // DH
    rows = BS // members
    order = sorted(range(1, members), reverse=True)
    arrived = []

    def exchange(take):
        got = [None] * members
        for d in order:
            earlier = arrived[-IN_FLIGHT:-IN_FLIGHT + 1] if len(arrived) >= IN_FLIGHT else []
            got[d] = lax.ppermute(
                take(d, *earlier), "context", [(i, i ^ d) for i in range(members)]
            )
            arrived.append(got[d])
        got[0] = take(0)
        return got

    def rows_of(array):
        return lambda d, *earlier: after(array, *earlier)[d * rows : (d + 1) * rows]

    def piece_of(pieces):
        return lambda d, *earlier: after(pieces[d], *earlier)

    def pooled(array):
        return (jnp.sum(array, axis=0, dtype=F32) / math.sqrt(BS)).astype(BF16)

    chosen = jnp.pad(selection[:, 0].astype(BF16), (0, width - heads))
    shared = jnp.stack([pooled(key_rows), chosen])[None]
    shared = lax.all_to_all(
        jnp.broadcast_to(shared, (members, 2, width)), "context", 0, 0, tiled=True
    )
    chosen = shared[:, 1, :heads].astype(jnp.int32)
    here = me.astype(jnp.int32)[None]

    held_k = exchange(rows_of(key_rows))
    held_v = exchange(rows_of(value_rows))
    own = own_part(after(query_rows, held_k[order[0]]), key_rows, value_rows)
    far_k = exchange(piece_of(pick_pieces(here, chosen, held_k)))
    far_v = exchange(piece_of(pick_pieces(here, chosen, held_v)))

    scaled, w = score_parts(query_rows, own, far_k)
    attended = finish(w, scaled, far_v)

    sort_logits = jnp.einsum(
        "hd,chd->hc",
        pooled(query_rows).reshape(heads, DH),
        shared[:, 0].reshape(members, heads, DH),
        preferred_element_type=F32,
    ) / math.sqrt(DH)
    return attended, sort_logits.reshape(heads, 1, members)


def solution(mesh):
    members = mesh.shape["context"]

    def per_device(query_rows, key_rows, value_rows, selection):
        fits = members & (members - 1) == 0 and BS % (16 * members) == 0
        if query_rows.shape[0] == BS and fits:
            return power_of_two(query_rows, key_rows, value_rows, selection)
        return any_size(query_rows, key_rows, value_rows, selection)

    placed = (
        P(("groups", "context"), "tensor"),
        P(("groups", "context"), "tensor"),
        P(("groups", "context"), "tensor"),
        P("tensor", ("groups", "context")),
    )
    return jax.shard_map(
        per_device,
        mesh=mesh,
        in_specs=placed,
        out_specs=(P(("groups", "context"), "tensor"), P("tensor", ("groups", "context"), None)),
        check_vma=False,
    )
```

```python
import functools
import math

import jax
import jax.numpy as jnp
from jax import lax
from jax.experimental import pallas as pl
from jax.experimental.pallas import tpu as pltpu
from jax.sharding import PartitionSpec as P

DH = 128
BS = 512
BF16 = jnp.bfloat16
F32 = jnp.float32


def block_partial(query_block, key_block, value_block):
    scores = jnp.dot(query_block, key_block.T, preferred_element_type=jnp.float32) * (
        1.0 / math.sqrt(DH)
    )
    row_max = jnp.max(scores, axis=1, keepdims=True)
    weights = jnp.exp(scores - row_max).astype(jnp.bfloat16)
    row_total = jnp.sum(weights.astype(jnp.float32), axis=1, keepdims=True)
    partial_sum = jnp.dot(weights, value_block, preferred_element_type=jnp.float32)
    return (row_max, row_total, partial_sum)


def combine_parts(own_part, far_part):
    own_max, own_total, own_sum = own_part
    far_max, far_total, far_sum = far_part
    joint = jnp.maximum(own_max, far_max)
    own_factor = jnp.exp(own_max - joint)
    far_factor = jnp.exp(far_max - joint)
    merged = (own_factor * own_sum + far_factor * far_sum) / (
        own_factor * own_total + far_factor * far_total
    )
    return merged.astype(jnp.bfloat16)


def any_size(query_rows, key_rows, value_rows, selection):
    members = lax.axis_size("context")
    tok_rows, width = query_rows.shape
    blocks = tok_rows // BS
    head_count = width // DH
    piece_rows = BS // members

    def pooled(rows_in):
        sums = jnp.sum(rows_in.reshape(blocks, BS, width), axis=1, dtype=jnp.float32) / math.sqrt(
            BS
        )
        return sums.astype(jnp.bfloat16).reshape(blocks, head_count, DH).transpose(1, 0, 2)

    pooled_q = pooled(query_rows)
    pooled_k = pooled(key_rows)
    products = jnp.einsum(
        "hbd,hcd->hbc",
        pooled_q,
        lax.all_gather(pooled_k, "context", axis=1, tiled=True),
        preferred_element_type=jnp.float32,
    )
    sort_logits = products / math.sqrt(DH)
    wanted = lax.all_gather(selection, "context", axis=1, tiled=True)
    query_grid = query_rows.reshape(blocks, BS, head_count, DH)
    key_grid = key_rows.reshape(blocks, BS, head_count, DH)
    value_grid = value_rows.reshape(blocks, BS, head_count, DH)
    pair_ids = jnp.arange(blocks * head_count, dtype=jnp.int32)

    def slice_pair(array, block, head):
        return lax.dynamic_slice(array, (block, 0, head, 0), (1, BS, 1, DH)).reshape(BS, DH)

    def pick_rows(held, table):
        inner = held.shape[-1] // head_count
        order_ids = table.reshape(head_count, members, blocks).transpose(2, 1, 0)
        source_dev = (order_ids // blocks)[:, :, None, :]
        source_blk = (order_ids % blocks)[:, :, None, :]
        row_ids = jnp.arange(piece_rows)[None, None, :, None]
        head_ids = jnp.arange(head_count)[None, None, None, :]
        grid = held.reshape(blocks, members, piece_rows, head_count, inner)
        return grid[source_blk, source_dev, row_ids, head_ids].reshape(
            blocks, members, piece_rows, head_count * inner
        )

    spread_k = key_rows.reshape(blocks, members, piece_rows, width)
    spread_v = value_rows.reshape(blocks, members, piece_rows, width)
    held_k = lax.all_to_all(spread_k, "context", split_axis=1, concat_axis=1, tiled=True)
    held_v = lax.all_to_all(spread_v, "context", split_axis=1, concat_axis=1, tiled=True)
    far_k = lax.all_to_all(
        pick_rows(held_k, wanted), "context", split_axis=1, concat_axis=1, tiled=True
    )
    far_v = lax.all_to_all(
        pick_rows(held_v, wanted), "context", split_axis=1, concat_axis=1, tiled=True
    )
    far_keys = far_k.reshape(blocks, BS, head_count, DH)
    far_values = far_v.reshape(blocks, BS, head_count, DH)

    def both_pair(pair_index):
        block = pair_index // head_count
        head = pair_index % head_count
        query_block = slice_pair(query_grid, block, head)
        own = block_partial(
            query_block, slice_pair(key_grid, block, head), slice_pair(value_grid, block, head)
        )
        far = block_partial(
            query_block, slice_pair(far_keys, block, head), slice_pair(far_values, block, head)
        )
        return combine_parts(own, far)

    outputs = lax.map(both_pair, pair_ids)
    attended = (
        outputs.reshape(blocks, head_count, BS, DH).transpose(0, 2, 1, 3).reshape(tok_rows, width)
    )
    return (attended, sort_logits)


def pick_kernel(members, heads, me_ref, chosen, *refs):
    pieces, outs, held = refs[:members], refs[members : 2 * members], refs[2 * members]
    me = me_ref[0]
    for e in range(members):
        held[e] = pieces[e][...]
    for d in range(members):
        for h in range(heads):
            cols = pl.ds(h * DH, DH)
            outs[d][:, cols] = held[me ^ chosen[d, h], :, cols]


def pick_pieces(me, chosen, pieces):
    members = len(pieces)
    rows, width = pieces[0].shape
    spec = pl.BlockSpec((rows, width), lambda i, m, t: (0, 0))
    return pl.pallas_call(
        functools.partial(pick_kernel, members, width // DH),
        grid_spec=pltpu.PrefetchScalarGridSpec(
            num_scalar_prefetch=2,
            grid=(1,),
            in_specs=[spec] * members,
            out_specs=[spec] * members,
            scratch_shapes=[pltpu.VMEM((members, rows, width), BF16)],
        ),
        out_shape=[jax.ShapeDtypeStruct((rows, width), BF16)] * members,
        cost_estimate=pl.CostEstimate(
            flops=0, transcendentals=0, bytes_accessed=4 * members * rows * width
        ),
    )(me, chosen, *pieces)


def stack_kernel(members, heads, me_ref, chosen, held, out):
    me = me_ref[0]
    for d in range(members):
        for h in range(heads):
            cols = pl.ds(h * DH, DH)
            out[me ^ d, :, cols] = held[chosen[d, h], :, cols]


def pick_stack(me, chosen, held):
    members, rows, width = held.shape
    spec = pl.BlockSpec((members, rows, width), lambda i, m, t: (0, 0, 0))
    return pl.pallas_call(
        functools.partial(stack_kernel, members, width // DH),
        grid_spec=pltpu.PrefetchScalarGridSpec(
            num_scalar_prefetch=2, grid=(1,), in_specs=[spec], out_specs=spec
        ),
        out_shape=jax.ShapeDtypeStruct((members, rows, width), BF16),
        cost_estimate=pl.CostEstimate(
            flops=0, transcendentals=0, bytes_accessed=4 * members * rows * width
        ),
    )(me, chosen, held)


def softmax_part(q, keys):
    s = lax.dot_general(q, keys, (((1,), (1,)), ((), ())), preferred_element_type=F32) * (
        1.0 / math.sqrt(DH)
    )
    top = jnp.max(s, axis=1, keepdims=True)
    w = jnp.exp(s - top).astype(BF16)
    return top, w, jnp.sum(w.astype(F32), axis=1, keepdims=True)


def own_kernel(q_ref, k_ref, v_ref, sum_ref, top_ref, total_ref):
    top, w, total = softmax_part(q_ref[...], k_ref[...])
    sum_ref[...] = jnp.dot(w, v_ref[...], preferred_element_type=F32)
    top_ref[0] = top
    total_ref[0] = total


def own_part(q, k, v):
    tok, width = q.shape
    heads = width // DH
    whole = pl.BlockSpec((tok, DH), lambda h: (0, h))
    column = pl.BlockSpec((1, tok, 1), lambda h: (h, 0, 0))
    return pl.pallas_call(
        own_kernel,
        grid=(heads,),
        in_specs=[whole] * 3,
        out_specs=[whole, column, column],
        out_shape=[
            jax.ShapeDtypeStruct((tok, width), F32),
            jax.ShapeDtypeStruct((heads, tok, 1), F32),
            jax.ShapeDtypeStruct((heads, tok, 1), F32),
        ],
        compiler_params=pltpu.CompilerParams(vmem_limit_bytes=16 << 20),
        cost_estimate=pl.CostEstimate(
            flops=4 * tok * BS * width,
            transcendentals=heads * tok * BS,
            bytes_accessed=10 * tok * width,
        ),
    )(q, k, v)


def scores_kernel(q_ref, sum_ref, top_ref, total_ref, far_k, own_ref, w_ref):
    far_max, far_w, far_total = softmax_part(q_ref[...], far_k[...].reshape(BS, DH))
    own_max = top_ref[0]
    joint = jnp.maximum(own_max, far_max)
    own_e = jnp.exp(own_max - joint)
    far_e = jnp.exp(far_max - joint)
    inverse = 1.0 / (own_e * total_ref[0] + far_e * far_total)
    own_ref[...] = sum_ref[...] * (own_e * inverse)
    w_ref[0] = (far_w.astype(F32) * (far_e * inverse)).astype(BF16)


def score_parts(q, own, far_k):
    members, rows, _ = far_k.shape
    tok, width = q.shape
    heads = width // DH
    whole = pl.BlockSpec((tok, DH), lambda h: (0, h))
    column = pl.BlockSpec((1, tok, 1), lambda h: (h, 0, 0))
    pieces = pl.BlockSpec((members, rows, DH), lambda h: (0, 0, h))
    return pl.pallas_call(
        scores_kernel,
        grid=(heads,),
        in_specs=[whole, whole, column, column, pieces],
        out_specs=[whole, pl.BlockSpec((1, tok, BS), lambda h: (h, 0, 0))],
        out_shape=[
            jax.ShapeDtypeStruct((tok, width), F32),
            jax.ShapeDtypeStruct((heads, tok, BS), BF16),
        ],
        compiler_params=pltpu.CompilerParams(vmem_limit_bytes=16 << 20),
        cost_estimate=pl.CostEstimate(
            flops=2 * tok * BS * width,
            transcendentals=heads * tok * BS,
            bytes_accessed=12 * tok * width + 2 * heads * tok * BS,
        ),
    )(q, *own, far_k)


def finish_kernel(members, me_ref, w_ref, own_ref, *refs):
    far_v, (out_ref, vf_ref) = refs[:members], refs[members:]
    rows = far_v[0].shape[0]
    for d in range(members):
        first = pl.multiple_of((me_ref[0] ^ d) * rows, rows)
        vf_ref[pl.ds(first, rows), :] = far_v[d][...]
    out_ref[...] = (
        own_ref[...] + jnp.dot(w_ref[0], vf_ref[...], preferred_element_type=F32)
    ).astype(BF16)


def finish(me, w, own, far_v):
    members = len(far_v)
    tok, width = own.shape
    heads = width // DH
    rows = far_v[0].shape[0]
    whole = pl.BlockSpec((tok, DH), lambda h, m: (0, h))
    piece = pl.BlockSpec((rows, DH), lambda h, m: (0, h))
    return pl.pallas_call(
        functools.partial(finish_kernel, members),
        grid_spec=pltpu.PrefetchScalarGridSpec(
            num_scalar_prefetch=1,
            grid=(heads,),
            in_specs=[pl.BlockSpec((1, tok, BS), lambda h, m: (h, 0, 0)), whole]
            + [piece] * members,
            out_specs=whole,
            scratch_shapes=[pltpu.VMEM((BS, DH), BF16)],
        ),
        out_shape=jax.ShapeDtypeStruct((tok, width), BF16),
        compiler_params=pltpu.CompilerParams(vmem_limit_bytes=16 << 20),
        cost_estimate=pl.CostEstimate(
            flops=2 * tok * BS * width,
            transcendentals=0,
            bytes_accessed=8 * tok * width + 2 * heads * tok * BS,
        ),
    )(me, w, own, *far_v)


def after(x, *earlier):
    return lax.optimization_barrier((x, *earlier))[0]


IN_FLIGHT = 5


def power_of_two(query_rows, key_rows, value_rows, selection):
    members = lax.axis_size("context")
    me = lax.axis_index("context")
    tok, width = query_rows.shape
    heads = width // DH
    rows = BS // members
    order = sorted(range(1, members), reverse=True)
    arrived = []

    def exchange(take):
        got = [None] * members
        for d in order:
            earlier = arrived[-IN_FLIGHT:-IN_FLIGHT + 1] if len(arrived) >= IN_FLIGHT else []
            got[d] = lax.ppermute(
                take(d, *earlier), "context", [(i, i ^ d) for i in range(members)]
            )
            arrived.append(got[d])
        got[0] = take(0)
        return got

    def rows_of(array):
        return lambda d, *earlier: lax.dynamic_slice_in_dim(
            after(array, *earlier), (me ^ d) * rows, rows
        )

    def piece_of(pieces):
        return lambda d, *earlier: after(pieces[d], *earlier)

    def swap(array):
        return lax.all_to_all(array, "context", 0, 0, tiled=True)

    def pooled(array):
        return (jnp.sum(array, axis=0, dtype=F32) / math.sqrt(BS)).astype(BF16)

    held_k = swap(key_rows.reshape(members, rows, width))

    chosen = jnp.pad(selection[:, 0].astype(BF16), (0, width - heads))
    mine = jnp.stack([pooled(key_rows), chosen])
    shared = jnp.stack(
        [mine]
        + [
            lax.ppermute(mine, "context", [(i, i ^ d) for i in range(members)])
            for d in range(1, members)
        ]
    )
    chosen = shared[:, 1, :heads].astype(jnp.int32)
    here = me.astype(jnp.int32)[None]

    held_v = exchange(rows_of(value_rows))
    own = own_part(after(query_rows, arrived[0]), key_rows, value_rows)
    far_k = swap(pick_stack(here, chosen, after(held_k, own[0], arrived[4])))
    far_v = exchange(piece_of(pick_pieces(here, chosen, held_v)))

    scaled, w = score_parts(query_rows, own, far_k)
    attended = finish(here, w, scaled, far_v)

    sort_logits = jnp.einsum(
        "hd,chd->hc",
        pooled(query_rows).reshape(heads, DH),
        shared[me ^ jnp.arange(members), 0].reshape(members, heads, DH),
        preferred_element_type=F32,
    ) / math.sqrt(DH)
    return attended, sort_logits.reshape(heads, 1, members)


def solution(mesh):
    members = mesh.shape["context"]

    def per_device(query_rows, key_rows, value_rows, selection):
        fits = members & (members - 1) == 0 and BS % (16 * members) == 0
        if query_rows.shape[0] == BS and fits:
            return power_of_two(query_rows, key_rows, value_rows, selection)
        return any_size(query_rows, key_rows, value_rows, selection)

    placed = (
        P(("groups", "context"), "tensor"),
        P(("groups", "context"), "tensor"),
        P(("groups", "context"), "tensor"),
        P("tensor", ("groups", "context")),
    )
    return jax.shard_map(
        per_device,
        mesh=mesh,
        in_specs=placed,
        out_specs=(P(("groups", "context"), "tensor"), P("tensor", ("groups", "context"), None)),
        check_vma=False,
    )
```

```python
import functools
import math

import jax
import jax.numpy as jnp
from jax import lax
from jax.experimental import pallas as pl
from jax.experimental.pallas import tpu as pltpu
from jax.sharding import PartitionSpec as P

DH = 128
BS = 512
BF16 = jnp.bfloat16
F32 = jnp.float32


def block_partial(query_block, key_block, value_block):
    scores = jnp.dot(query_block, key_block.T, preferred_element_type=jnp.float32) * (
        1.0 / math.sqrt(DH)
    )
    row_max = jnp.max(scores, axis=1, keepdims=True)
    weights = jnp.exp(scores - row_max).astype(jnp.bfloat16)
    row_total = jnp.sum(weights.astype(jnp.float32), axis=1, keepdims=True)
    partial_sum = jnp.dot(weights, value_block, preferred_element_type=jnp.float32)
    return (row_max, row_total, partial_sum)


def combine_parts(own_part, far_part):
    own_max, own_total, own_sum = own_part
    far_max, far_total, far_sum = far_part
    joint = jnp.maximum(own_max, far_max)
    own_factor = jnp.exp(own_max - joint)
    far_factor = jnp.exp(far_max - joint)
    merged = (own_factor * own_sum + far_factor * far_sum) / (
        own_factor * own_total + far_factor * far_total
    )
    return merged.astype(jnp.bfloat16)


def any_size(query_rows, key_rows, value_rows, selection):
    members = lax.axis_size("context")
    tok_rows, width = query_rows.shape
    blocks = tok_rows // BS
    head_count = width // DH
    piece_rows = BS // members

    def pooled(rows_in):
        sums = jnp.sum(rows_in.reshape(blocks, BS, width), axis=1, dtype=jnp.float32) / math.sqrt(
            BS
        )
        return sums.astype(jnp.bfloat16).reshape(blocks, head_count, DH).transpose(1, 0, 2)

    pooled_q = pooled(query_rows)
    pooled_k = pooled(key_rows)
    products = jnp.einsum(
        "hbd,hcd->hbc",
        pooled_q,
        lax.all_gather(pooled_k, "context", axis=1, tiled=True),
        preferred_element_type=jnp.float32,
    )
    sort_logits = products / math.sqrt(DH)
    wanted = lax.all_gather(selection, "context", axis=1, tiled=True)
    query_grid = query_rows.reshape(blocks, BS, head_count, DH)
    key_grid = key_rows.reshape(blocks, BS, head_count, DH)
    value_grid = value_rows.reshape(blocks, BS, head_count, DH)
    pair_ids = jnp.arange(blocks * head_count, dtype=jnp.int32)

    def slice_pair(array, block, head):
        return lax.dynamic_slice(array, (block, 0, head, 0), (1, BS, 1, DH)).reshape(BS, DH)

    def pick_rows(held, table):
        inner = held.shape[-1] // head_count
        order_ids = table.reshape(head_count, members, blocks).transpose(2, 1, 0)
        source_dev = (order_ids // blocks)[:, :, None, :]
        source_blk = (order_ids % blocks)[:, :, None, :]
        row_ids = jnp.arange(piece_rows)[None, None, :, None]
        head_ids = jnp.arange(head_count)[None, None, None, :]
        grid = held.reshape(blocks, members, piece_rows, head_count, inner)
        return grid[source_blk, source_dev, row_ids, head_ids].reshape(
            blocks, members, piece_rows, head_count * inner
        )

    spread_k = key_rows.reshape(blocks, members, piece_rows, width)
    spread_v = value_rows.reshape(blocks, members, piece_rows, width)
    held_k = lax.all_to_all(spread_k, "context", split_axis=1, concat_axis=1, tiled=True)
    held_v = lax.all_to_all(spread_v, "context", split_axis=1, concat_axis=1, tiled=True)
    far_k = lax.all_to_all(
        pick_rows(held_k, wanted), "context", split_axis=1, concat_axis=1, tiled=True
    )
    far_v = lax.all_to_all(
        pick_rows(held_v, wanted), "context", split_axis=1, concat_axis=1, tiled=True
    )
    far_keys = far_k.reshape(blocks, BS, head_count, DH)
    far_values = far_v.reshape(blocks, BS, head_count, DH)

    def both_pair(pair_index):
        block = pair_index // head_count
        head = pair_index % head_count
        query_block = slice_pair(query_grid, block, head)
        own = block_partial(
            query_block, slice_pair(key_grid, block, head), slice_pair(value_grid, block, head)
        )
        far = block_partial(
            query_block, slice_pair(far_keys, block, head), slice_pair(far_values, block, head)
        )
        return combine_parts(own, far)

    outputs = lax.map(both_pair, pair_ids)
    attended = (
        outputs.reshape(blocks, head_count, BS, DH).transpose(0, 2, 1, 3).reshape(tok_rows, width)
    )
    return (attended, sort_logits)


SCALE = math.log2(math.e) / math.sqrt(DH)
EXTRA = 16


def pack_kernel(heads, k_ref, chosen_ref, out_ref):
    sums = jnp.sum(k_ref[...].astype(F32), axis=0, keepdims=True) / math.sqrt(BS)
    pooled = sums.astype(BF16)
    rows = jnp.concatenate([pooled[:, h * DH : (h + 1) * DH] for h in range(heads)], axis=0)
    for h in range(heads):
        out_ref[h, pl.ds(0, BS), :] = k_ref[:, pl.ds(h * DH, DH)]
        out_ref[h, pl.ds(BS, EXTRA), :] = jnp.concatenate(
            [rows, jnp.broadcast_to(chosen_ref[pl.ds(h, 1), :], (EXTRA - heads, DH))], axis=0
        )


def pack_keys(k, chosen):
    tok, width = k.shape
    heads = width // DH
    return pl.pallas_call(
        functools.partial(pack_kernel, heads),
        out_shape=jax.ShapeDtypeStruct((heads, BS + EXTRA, DH), BF16),
        compiler_params=pltpu.CompilerParams(vmem_limit_bytes=16 << 20),
        cost_estimate=pl.CostEstimate(
            flops=tok * width, transcendentals=0, bytes_accessed=4 * tok * width
        ),
    )(k, chosen)


def split_kernel(heads, v_ref, out_ref):
    for h in range(heads):
        out_ref[h] = v_ref[:, pl.ds(h * DH, DH)]


def split_heads(v):
    tok, width = v.shape
    heads = width // DH
    return pl.pallas_call(
        functools.partial(split_kernel, heads),
        out_shape=jax.ShapeDtypeStruct((heads, tok, DH), BF16),
        compiler_params=pltpu.CompilerParams(vmem_limit_bytes=16 << 20),
        cost_estimate=pl.CostEstimate(
            flops=0, transcendentals=0, bytes_accessed=4 * tok * width
        ),
    )(v)


def attend_kernel(me_ref, chosen, q_ref, ko_ref, kf_ref, vo_ref, vf_ref, out_ref):
    q = q_ref[...]

    def part(keys, values):
        s = lax.dot_general(q, keys, (((1,), (1,)), ((), ())), preferred_element_type=F32)
        top = jnp.max(s, axis=1, keepdims=True) * SCALE
        w = jnp.exp2(s * SCALE - top).astype(BF16)
        total = jnp.sum(w.astype(F32), axis=1, keepdims=True)
        return top, total, jnp.dot(w, values, preferred_element_type=F32)

    own_max, own_total, own_sum = part(ko_ref[0], vo_ref[0])
    far_max, far_total, far_sum = part(kf_ref[0], vf_ref[0])
    joint = jnp.maximum(own_max, far_max)
    own_e = jnp.exp2(own_max - joint)
    far_e = jnp.exp2(far_max - joint)
    inverse = 1.0 / (own_e * own_total + far_e * far_total)
    out_ref[...] = ((own_e * inverse) * own_sum + (far_e * inverse) * far_sum).astype(BF16)


def attend(me, chosen, d, q, keys, values):
    own = pl.BlockSpec((1, BS, DH), lambda i, m, t: (m[0] ^ d, 0, 0))
    far = pl.BlockSpec((1, BS, DH), lambda i, m, t: (t[m[0] ^ d], 0, 0))
    rows = pl.BlockSpec((BS, DH), lambda i, m, t: (0, 0))
    return pl.pallas_call(
        attend_kernel,
        grid_spec=pltpu.PrefetchScalarGridSpec(
            num_scalar_prefetch=2,
            grid=(1,),
            in_specs=[rows, own, far, own, far],
            out_specs=rows,
        ),
        out_shape=jax.ShapeDtypeStruct((BS, DH), BF16),
        compiler_params=pltpu.CompilerParams(vmem_limit_bytes=16 << 20),
        cost_estimate=pl.CostEstimate(
            flops=8 * BS * BS * DH, transcendentals=2 * BS * BS, bytes_accessed=12 * BS * DH
        ),
    )(me, chosen, q, keys, keys, values, values)


def join_kernel(members, me_ref, *refs):
    pieces, out_ref = refs[:members], refs[members]
    for d in range(members):
        first = pl.multiple_of((me_ref[0] ^ d) * DH, DH)
        out_ref[:, pl.ds(first, DH)] = pieces[d][...]


def join_heads(me, pieces):
    members = len(pieces)
    tok = pieces[0].shape[0]
    piece = pl.BlockSpec((tok, DH), lambda i, m: (0, 0))
    return pl.pallas_call(
        functools.partial(join_kernel, members),
        grid_spec=pltpu.PrefetchScalarGridSpec(
            num_scalar_prefetch=1,
            grid=(1,),
            in_specs=[piece] * members,
            out_specs=pl.BlockSpec((tok, members * DH), lambda i, m: (0, 0)),
        ),
        out_shape=jax.ShapeDtypeStruct((tok, members * DH), BF16),
        compiler_params=pltpu.CompilerParams(vmem_limit_bytes=16 << 20),
        cost_estimate=pl.CostEstimate(
            flops=0, transcendentals=0, bytes_accessed=4 * members * tok * DH
        ),
    )(me, *pieces)


def after(x, *earlier):
    return lax.optimization_barrier((x, *earlier))[0]


IN_FLIGHT = 5
BEFORE_VALUES = 5


def by_heads(query_rows, key_rows, value_rows, selection):
    members = lax.axis_size("context")
    me = lax.axis_index("context")
    tok, width = query_rows.shape
    heads = width // DH
    order = sorted(range(1, members), reverse=True)

    def send(x, d):
        return lax.ppermute(x, "context", [(i, i ^ d) for i in range(members)])

    def swap(array):
        return lax.all_to_all(array, "context", 0, 0, tiled=True)

    def columns(array, d):
        return lax.dynamic_slice_in_dim(array, (me ^ d) * DH, DH, axis=1)

    chosen = jnp.broadcast_to(selection.astype(BF16), (heads, DH))
    keys = swap(pack_keys(key_rows, chosen))
    queries = [None] * members
    arrived = []
    for n, d in enumerate(order):
        earlier = arrived[n - IN_FLIGHT : n - IN_FLIGHT + 1] if n >= IN_FLIGHT else []
        queries[d] = send(columns(after(query_rows, *earlier), d), d)
        arrived.append(queries[d])
    queries[0] = columns(query_rows, 0)
    values = swap(after(split_heads(value_rows), keys, *arrived[:BEFORE_VALUES]))

    chosen = keys[:, BS + heads, 0].astype(jnp.int32)
    here = me.astype(jnp.int32)[None]
    outputs = [None] * members
    for d in order + [0]:
        outputs[d] = attend(here, chosen, d, queries[d], keys, values)
        if d:
            outputs[d] = send(outputs[d], d)
    attended = join_heads(here, outputs)

    pooled_q = (jnp.sum(query_rows, axis=0, dtype=F32) / math.sqrt(BS)).astype(BF16)
    sort_logits = jnp.einsum(
        "hd,chd->hc",
        pooled_q.reshape(heads, DH),
        keys[:, BS : BS + heads],
        preferred_element_type=F32,
    ) / math.sqrt(DH)
    return attended, sort_logits.reshape(heads, 1, members)


def solution(mesh):
    members = mesh.shape["context"]

    def per_device(query_rows, key_rows, value_rows, selection):
        tok, width = query_rows.shape
        fits = tok == BS and width == members * DH and members & (members - 1) == 0
        if fits and members < EXTRA:
            return by_heads(query_rows, key_rows, value_rows, selection)
        return any_size(query_rows, key_rows, value_rows, selection)

    placed = (
        P(("groups", "context"), "tensor"),
        P(("groups", "context"), "tensor"),
        P(("groups", "context"), "tensor"),
        P("tensor", ("groups", "context")),
    )
    return jax.shard_map(
        per_device,
        mesh=mesh,
        in_specs=placed,
        out_specs=(P(("groups", "context"), "tensor"), P("tensor", ("groups", "context"), None)),
        check_vma=False,
    )
```

```python
import functools
import math

import jax
import jax.numpy as jnp
from jax import lax
from jax.experimental import pallas as pl
from jax.experimental.pallas import tpu as pltpu
from jax.sharding import PartitionSpec as P

DH = 128
BS = 512
BF16 = jnp.bfloat16
F32 = jnp.float32


def block_partial(query_block, key_block, value_block):
    scores = jnp.dot(query_block, key_block.T, preferred_element_type=jnp.float32) * (
        1.0 / math.sqrt(DH)
    )
    row_max = jnp.max(scores, axis=1, keepdims=True)
    weights = jnp.exp(scores - row_max).astype(jnp.bfloat16)
    row_total = jnp.sum(weights.astype(jnp.float32), axis=1, keepdims=True)
    partial_sum = jnp.dot(weights, value_block, preferred_element_type=jnp.float32)
    return (row_max, row_total, partial_sum)


def combine_parts(own_part, far_part):
    own_max, own_total, own_sum = own_part
    far_max, far_total, far_sum = far_part
    joint = jnp.maximum(own_max, far_max)
    own_factor = jnp.exp(own_max - joint)
    far_factor = jnp.exp(far_max - joint)
    merged = (own_factor * own_sum + far_factor * far_sum) / (
        own_factor * own_total + far_factor * far_total
    )
    return merged.astype(jnp.bfloat16)


def any_size(query_rows, key_rows, value_rows, selection):
    members = lax.axis_size("context")
    tok_rows, width = query_rows.shape
    blocks = tok_rows // BS
    head_count = width // DH
    piece_rows = BS // members

    def pooled(rows_in):
        sums = jnp.sum(rows_in.reshape(blocks, BS, width), axis=1, dtype=jnp.float32) / math.sqrt(
            BS
        )
        return sums.astype(jnp.bfloat16).reshape(blocks, head_count, DH).transpose(1, 0, 2)

    pooled_q = pooled(query_rows)
    pooled_k = pooled(key_rows)
    products = jnp.einsum(
        "hbd,hcd->hbc",
        pooled_q,
        lax.all_gather(pooled_k, "context", axis=1, tiled=True),
        preferred_element_type=jnp.float32,
    )
    sort_logits = products / math.sqrt(DH)
    wanted = lax.all_gather(selection, "context", axis=1, tiled=True)
    query_grid = query_rows.reshape(blocks, BS, head_count, DH)
    key_grid = key_rows.reshape(blocks, BS, head_count, DH)
    value_grid = value_rows.reshape(blocks, BS, head_count, DH)
    pair_ids = jnp.arange(blocks * head_count, dtype=jnp.int32)

    def slice_pair(array, block, head):
        return lax.dynamic_slice(array, (block, 0, head, 0), (1, BS, 1, DH)).reshape(BS, DH)

    def pick_rows(held, table):
        inner = held.shape[-1] // head_count
        order_ids = table.reshape(head_count, members, blocks).transpose(2, 1, 0)
        source_dev = (order_ids // blocks)[:, :, None, :]
        source_blk = (order_ids % blocks)[:, :, None, :]
        row_ids = jnp.arange(piece_rows)[None, None, :, None]
        head_ids = jnp.arange(head_count)[None, None, None, :]
        grid = held.reshape(blocks, members, piece_rows, head_count, inner)
        return grid[source_blk, source_dev, row_ids, head_ids].reshape(
            blocks, members, piece_rows, head_count * inner
        )

    spread_k = key_rows.reshape(blocks, members, piece_rows, width)
    spread_v = value_rows.reshape(blocks, members, piece_rows, width)
    held_k = lax.all_to_all(spread_k, "context", split_axis=1, concat_axis=1, tiled=True)
    held_v = lax.all_to_all(spread_v, "context", split_axis=1, concat_axis=1, tiled=True)
    far_k = lax.all_to_all(
        pick_rows(held_k, wanted), "context", split_axis=1, concat_axis=1, tiled=True
    )
    far_v = lax.all_to_all(
        pick_rows(held_v, wanted), "context", split_axis=1, concat_axis=1, tiled=True
    )
    far_keys = far_k.reshape(blocks, BS, head_count, DH)
    far_values = far_v.reshape(blocks, BS, head_count, DH)

    def both_pair(pair_index):
        block = pair_index // head_count
        head = pair_index % head_count
        query_block = slice_pair(query_grid, block, head)
        own = block_partial(
            query_block, slice_pair(key_grid, block, head), slice_pair(value_grid, block, head)
        )
        far = block_partial(
            query_block, slice_pair(far_keys, block, head), slice_pair(far_values, block, head)
        )
        return combine_parts(own, far)

    outputs = lax.map(both_pair, pair_ids)
    attended = (
        outputs.reshape(blocks, head_count, BS, DH).transpose(0, 2, 1, 3).reshape(tok_rows, width)
    )
    return (attended, sort_logits)


SCALE = math.log2(math.e) / math.sqrt(DH)
TILE = 8


def pack_kernel(me_ref, k_ref, v_ref, out_ref):
    out_ref[pl.ds(0, BS), :] = k_ref[...]
    out_ref[pl.ds(BS, BS), :] = v_ref[...]


def pack_head(me, d, k, v):
    rows = 2 * BS
    part = pl.BlockSpec((BS, DH), lambda i, m: (0, m[0] ^ d))
    return pl.pallas_call(
        pack_kernel,
        grid_spec=pltpu.PrefetchScalarGridSpec(
            num_scalar_prefetch=1,
            grid=(1,),
            in_specs=[part, part],
            out_specs=pl.BlockSpec((rows, DH), lambda i, m: (0, 0)),
        ),
        out_shape=jax.ShapeDtypeStruct((rows, DH), BF16),
        cost_estimate=pl.CostEstimate(
            flops=0, transcendentals=0, bytes_accessed=4 * rows * DH
        ),
    )(me, k, v)


def pooled(array):
    return (jnp.sum(array.astype(F32), axis=0, keepdims=True) / math.sqrt(BS)).astype(BF16)


def cut_kernel(heads, me_ref, q_ref, k_ref, chosen_ref, pooled_ref, *pieces):
    def by_head(row):
        return jnp.concatenate([row[:, h * DH : (h + 1) * DH] for h in range(heads)], axis=0)

    pooled_ref[...] = by_head(pooled(q_ref[...]))
    pooled_keys = by_head(pooled(k_ref[...]))
    for d in range(heads):
        first = pl.multiple_of((me_ref[0] ^ d) * DH, DH)
        pieces[d][pl.ds(0, BS), :] = q_ref[:, pl.ds(first, DH)]
        pieces[d][pl.ds(BS, heads), :] = pooled_keys
        pieces[d][pl.ds(BS + heads, TILE), :] = chosen_ref[me_ref[0] ^ d]


def cut_queries(me, q, k, chosen):
    tok, width = q.shape
    heads = width // DH
    whole = pl.BlockSpec((tok, width), lambda i, m: (0, 0))
    piece = pl.BlockSpec((tok + heads + TILE, DH), lambda i, m: (0, 0))
    return pl.pallas_call(
        functools.partial(cut_kernel, heads),
        grid_spec=pltpu.PrefetchScalarGridSpec(
            num_scalar_prefetch=1,
            grid=(1,),
            in_specs=[whole, whole, pl.BlockSpec((heads, TILE, DH), lambda i, m: (0, 0, 0))],
            out_specs=[pl.BlockSpec((heads, DH), lambda i, m: (0, 0))] + [piece] * heads,
        ),
        out_shape=[jax.ShapeDtypeStruct((heads, DH), BF16)]
        + [jax.ShapeDtypeStruct((tok + heads + TILE, DH), BF16)] * heads,
        compiler_params=pltpu.CompilerParams(vmem_limit_bytes=24 << 20),
        cost_estimate=pl.CostEstimate(
            flops=2 * tok * width, transcendentals=0, bytes_accessed=6 * tok * width
        ),
    )(me, q, k, chosen)


def logits_kernel(heads, me_ref, pooled_ref, *refs):
    pieces, out_ref = refs[:heads], refs[heads]
    q = pooled_ref[...].astype(F32)
    lane = lax.broadcasted_iota(jnp.int32, (heads, heads), 1)
    logits = jnp.zeros((heads, heads), F32)
    for d in range(heads):
        one = jnp.sum(q * pieces[d][...].astype(F32), axis=1, keepdims=True)
        logits = jnp.where(lane == (me_ref[0] ^ d), one / math.sqrt(DH), logits)
    out_ref[...] = logits


def logits_of(me, pooled_q, pieces):
    heads = len(pieces)
    rows = pl.BlockSpec((heads, DH), lambda i, m: (BS // heads, 0))
    return pl.pallas_call(
        functools.partial(logits_kernel, heads),
        grid_spec=pltpu.PrefetchScalarGridSpec(
            num_scalar_prefetch=1,
            grid=(1,),
            in_specs=[pl.BlockSpec((heads, DH), lambda i, m: (0, 0))] + [rows] * heads,
            out_specs=pl.BlockSpec((heads, heads), lambda i, m: (0, 0)),
        ),
        out_shape=jax.ShapeDtypeStruct((heads, heads), F32),
    )(me, pooled_q, *pieces)


def attend_kernel(me_ref, q_ref, tile_ref, k_ref, v_ref, *refs):
    packed, (out_ref, far_ref, sem) = refs[:-3], refs[-3:]
    source = me_ref[0] ^ jnp.max(tile_ref[...].astype(F32)).astype(jnp.int32)
    copies = [pltpu.make_async_copy(one, far_ref, sem) for one in packed]
    for n, copy in enumerate(copies):
        pl.when(source == n)(copy.start)
    q = q_ref[...]

    def part(keys, values):
        s = lax.dot_general(q, keys, (((1,), (1,)), ((), ())), preferred_element_type=F32)
        top = jnp.max(s, axis=1, keepdims=True) * SCALE
        w = jnp.exp2(s * SCALE - top).astype(BF16)
        total = jnp.sum(w.astype(F32), axis=1, keepdims=True)
        return top, total, jnp.dot(w, values, preferred_element_type=F32)

    own_max, own_total, own_sum = part(k_ref[...], v_ref[...])
    copies[0].wait()
    far_max, far_total, far_sum = part(far_ref[pl.ds(0, BS), :], far_ref[pl.ds(BS, BS), :])
    joint = jnp.maximum(own_max, far_max)
    own_e = jnp.exp2(own_max - joint)
    far_e = jnp.exp2(far_max - joint)
    inverse = 1.0 / (own_e * own_total + far_e * far_total)
    out_ref[...] = ((own_e * inverse) * own_sum + (far_e * inverse) * far_sum).astype(BF16)


def attend(me, d, q, packed):
    def rows(n):
        return pl.BlockSpec((BS, DH), lambda i, m: (n, 0))

    return pl.pallas_call(
        attend_kernel,
        grid_spec=pltpu.PrefetchScalarGridSpec(
            num_scalar_prefetch=1,
            grid=(1,),
            in_specs=[
                rows(0),
                pl.BlockSpec((TILE, DH), lambda i, m: (q.shape[0] // TILE - 1, 0)),
                rows(0),
                rows(1),
            ]
            + [pl.BlockSpec(memory_space=pl.ANY)] * len(packed),
            out_specs=rows(0),
            scratch_shapes=[pltpu.VMEM((2 * BS, DH), BF16), pltpu.SemaphoreType.DMA],
        ),
        out_shape=jax.ShapeDtypeStruct((BS, DH), BF16),
        compiler_params=pltpu.CompilerParams(vmem_limit_bytes=16 << 20),
        cost_estimate=pl.CostEstimate(
            flops=8 * BS * BS * DH, transcendentals=2 * BS * BS, bytes_accessed=12 * BS * DH
        ),
    )(me, q, q, packed[d], packed[d], *packed)


def join_kernel(members, me_ref, *refs):
    pieces, out_ref = refs[:members], refs[members]
    for d in range(members):
        first = pl.multiple_of((me_ref[0] ^ d) * DH, DH)
        out_ref[:, pl.ds(first, DH)] = pieces[d][...]


def join_heads(me, pieces):
    members = len(pieces)
    tok = pieces[0].shape[0]
    piece = pl.BlockSpec((tok, DH), lambda i, m: (0, 0))
    return pl.pallas_call(
        functools.partial(join_kernel, members),
        grid_spec=pltpu.PrefetchScalarGridSpec(
            num_scalar_prefetch=1,
            grid=(1,),
            in_specs=[piece] * members,
            out_specs=pl.BlockSpec((tok, members * DH), lambda i, m: (0, 0)),
        ),
        out_shape=jax.ShapeDtypeStruct((tok, members * DH), BF16),
        compiler_params=pltpu.CompilerParams(vmem_limit_bytes=16 << 20),
        cost_estimate=pl.CostEstimate(
            flops=0, transcendentals=0, bytes_accessed=4 * members * tok * DH
        ),
    )(me, *pieces)


def after(x, *earlier):
    return lax.optimization_barrier((x, *earlier))[0]


IN_FLIGHT = 5


def by_heads(query_rows, key_rows, value_rows, selection):
    members = lax.axis_size("context")
    me = lax.axis_index("context")
    tok, width = query_rows.shape
    heads = width // DH
    here = me.astype(jnp.int32)[None]
    near = list(range(1, members // 2))
    far = list(range(members // 2, members))
    arrived = []

    def exchange(pieces, order):
        got = list(pieces)
        for d in order:
            earlier = arrived[-IN_FLIGHT:][:1] if len(arrived) >= IN_FLIGHT else []
            got[d] = lax.ppermute(
                after(pieces[d], *earlier), "context", [(i, i ^ d) for i in range(members)]
            )
            arrived.append(got[d])
        return got

    packed = [pack_head(here, d, key_rows, value_rows) for d in range(members)]
    packed = exchange(packed, far[::-1] + near)
    chosen = jnp.broadcast_to(selection.astype(BF16)[:, :, None], (heads, TILE, DH))
    pooled_q, *pieces = cut_queries(here, after(query_rows, arrived[0]), key_rows, chosen)
    queries = exchange(pieces, far[::-1] + near)
    sort_logits = logits_of(here, pooled_q, queries)

    outputs = [None] * members
    for d in far[::-1] + near + [0]:
        outputs[d] = attend(here, d, queries[d], packed)
        if d:
            outputs[d] = lax.ppermute(
                outputs[d], "context", [(i, i ^ d) for i in range(members)]
            )
    attended = join_heads(here, outputs)
    return attended, sort_logits.reshape(heads, 1, members)


def solution(mesh):
    members = mesh.shape["context"]

    def per_device(query_rows, key_rows, value_rows, selection):
        tok, width = query_rows.shape
        fits = tok == BS and width == members * DH and members & (members - 1) == 0
        if fits and members == TILE:
            return by_heads(query_rows, key_rows, value_rows, selection)
        return any_size(query_rows, key_rows, value_rows, selection)

    placed = (
        P(("groups", "context"), "tensor"),
        P(("groups", "context"), "tensor"),
        P(("groups", "context"), "tensor"),
        P("tensor", ("groups", "context")),
    )
    return jax.shard_map(
        per_device,
        mesh=mesh,
        in_specs=placed,
        out_specs=(P(("groups", "context"), "tensor"), P("tensor", ("groups", "context"), None)),
        check_vma=False,
    )
```

```python
import functools
import math

import jax
import jax.numpy as jnp
from jax import lax
from jax.experimental import pallas as pl
from jax.experimental.pallas import tpu as pltpu
from jax.sharding import PartitionSpec as P

DH = 128
BS = 512
BF16 = jnp.bfloat16
F32 = jnp.float32


def block_partial(query_block, key_block, value_block):
    scores = jnp.dot(query_block, key_block.T, preferred_element_type=jnp.float32) * (
        1.0 / math.sqrt(DH)
    )
    row_max = jnp.max(scores, axis=1, keepdims=True)
    weights = jnp.exp(scores - row_max).astype(jnp.bfloat16)
    row_total = jnp.sum(weights.astype(jnp.float32), axis=1, keepdims=True)
    partial_sum = jnp.dot(weights, value_block, preferred_element_type=jnp.float32)
    return (row_max, row_total, partial_sum)


def combine_parts(own_part, far_part):
    own_max, own_total, own_sum = own_part
    far_max, far_total, far_sum = far_part
    joint = jnp.maximum(own_max, far_max)
    own_factor = jnp.exp(own_max - joint)
    far_factor = jnp.exp(far_max - joint)
    merged = (own_factor * own_sum + far_factor * far_sum) / (
        own_factor * own_total + far_factor * far_total
    )
    return merged.astype(jnp.bfloat16)


def any_size(query_rows, key_rows, value_rows, selection):
    members = lax.axis_size("context")
    tok_rows, width = query_rows.shape
    blocks = tok_rows // BS
    head_count = width // DH
    piece_rows = BS // members

    def pooled(rows_in):
        sums = jnp.sum(rows_in.reshape(blocks, BS, width), axis=1, dtype=jnp.float32) / math.sqrt(
            BS
        )
        return sums.astype(jnp.bfloat16).reshape(blocks, head_count, DH).transpose(1, 0, 2)

    pooled_q = pooled(query_rows)
    pooled_k = pooled(key_rows)
    products = jnp.einsum(
        "hbd,hcd->hbc",
        pooled_q,
        lax.all_gather(pooled_k, "context", axis=1, tiled=True),
        preferred_element_type=jnp.float32,
    )
    sort_logits = products / math.sqrt(DH)
    wanted = lax.all_gather(selection, "context", axis=1, tiled=True)
    query_grid = query_rows.reshape(blocks, BS, head_count, DH)
    key_grid = key_rows.reshape(blocks, BS, head_count, DH)
    value_grid = value_rows.reshape(blocks, BS, head_count, DH)
    pair_ids = jnp.arange(blocks * head_count, dtype=jnp.int32)

    def slice_pair(array, block, head):
        return lax.dynamic_slice(array, (block, 0, head, 0), (1, BS, 1, DH)).reshape(BS, DH)

    def pick_rows(held, table):
        inner = held.shape[-1] // head_count
        order_ids = table.reshape(head_count, members, blocks).transpose(2, 1, 0)
        source_dev = (order_ids // blocks)[:, :, None, :]
        source_blk = (order_ids % blocks)[:, :, None, :]
        row_ids = jnp.arange(piece_rows)[None, None, :, None]
        head_ids = jnp.arange(head_count)[None, None, None, :]
        grid = held.reshape(blocks, members, piece_rows, head_count, inner)
        return grid[source_blk, source_dev, row_ids, head_ids].reshape(
            blocks, members, piece_rows, head_count * inner
        )

    spread_k = key_rows.reshape(blocks, members, piece_rows, width)
    spread_v = value_rows.reshape(blocks, members, piece_rows, width)
    held_k = lax.all_to_all(spread_k, "context", split_axis=1, concat_axis=1, tiled=True)
    held_v = lax.all_to_all(spread_v, "context", split_axis=1, concat_axis=1, tiled=True)
    far_k = lax.all_to_all(
        pick_rows(held_k, wanted), "context", split_axis=1, concat_axis=1, tiled=True
    )
    far_v = lax.all_to_all(
        pick_rows(held_v, wanted), "context", split_axis=1, concat_axis=1, tiled=True
    )
    far_keys = far_k.reshape(blocks, BS, head_count, DH)
    far_values = far_v.reshape(blocks, BS, head_count, DH)

    def both_pair(pair_index):
        block = pair_index // head_count
        head = pair_index % head_count
        query_block = slice_pair(query_grid, block, head)
        own = block_partial(
            query_block, slice_pair(key_grid, block, head), slice_pair(value_grid, block, head)
        )
        far = block_partial(
            query_block, slice_pair(far_keys, block, head), slice_pair(far_values, block, head)
        )
        return combine_parts(own, far)

    outputs = lax.map(both_pair, pair_ids)
    attended = (
        outputs.reshape(blocks, head_count, BS, DH).transpose(0, 2, 1, 3).reshape(tok_rows, width)
    )
    return (attended, sort_logits)


SCALE = math.log2(math.e) / math.sqrt(DH)
TILE = 8


def pack_kernel(me_ref, k_ref, v_ref, out_ref):
    out_ref[pl.ds(0, BS), :] = k_ref[...]
    out_ref[pl.ds(BS, BS), :] = v_ref[...]


def pack_head(me, d, k, v):
    rows = 2 * BS
    part = pl.BlockSpec((BS, DH), lambda i, m: (0, m[0] ^ d))
    return pl.pallas_call(
        pack_kernel,
        grid_spec=pltpu.PrefetchScalarGridSpec(
            num_scalar_prefetch=1,
            grid=(1,),
            in_specs=[part, part],
            out_specs=pl.BlockSpec((rows, DH), lambda i, m: (0, 0)),
        ),
        out_shape=jax.ShapeDtypeStruct((rows, DH), BF16),
        cost_estimate=pl.CostEstimate(
            flops=0, transcendentals=0, bytes_accessed=4 * rows * DH
        ),
    )(me, k, v)


def pooled(array):
    return (jnp.sum(array.astype(F32), axis=0, keepdims=True) / math.sqrt(BS)).astype(BF16)


def cut_kernel(heads, me_ref, q_ref, k_ref, chosen_ref, pooled_ref, *pieces):
    def by_head(row):
        return jnp.concatenate([row[:, h * DH : (h + 1) * DH] for h in range(heads)], axis=0)

    pooled_ref[...] = by_head(pooled(q_ref[...]))
    pooled_keys = by_head(pooled(k_ref[...]))
    for d in range(heads):
        first = pl.multiple_of((me_ref[0] ^ d) * DH, DH)
        pieces[d][pl.ds(0, BS), :] = q_ref[:, pl.ds(first, DH)]
        pieces[d][pl.ds(BS, heads), :] = pooled_keys
        pieces[d][pl.ds(BS + heads, TILE), :] = chosen_ref[me_ref[0] ^ d]


def cut_queries(me, q, k, chosen):
    tok, width = q.shape
    heads = width // DH
    whole = pl.BlockSpec((tok, width), lambda i, m: (0, 0))
    piece = pl.BlockSpec((tok + heads + TILE, DH), lambda i, m: (0, 0))
    return pl.pallas_call(
        functools.partial(cut_kernel, heads),
        grid_spec=pltpu.PrefetchScalarGridSpec(
            num_scalar_prefetch=1,
            grid=(1,),
            in_specs=[whole, whole, pl.BlockSpec((heads, TILE, DH), lambda i, m: (0, 0, 0))],
            out_specs=[pl.BlockSpec((heads, DH), lambda i, m: (0, 0))] + [piece] * heads,
        ),
        out_shape=[jax.ShapeDtypeStruct((heads, DH), BF16)]
        + [jax.ShapeDtypeStruct((tok + heads + TILE, DH), BF16)] * heads,
        compiler_params=pltpu.CompilerParams(vmem_limit_bytes=24 << 20),
        cost_estimate=pl.CostEstimate(
            flops=2 * tok * width, transcendentals=0, bytes_accessed=6 * tok * width
        ),
    )(me, q, k, chosen)


def logits_kernel(heads, me_ref, pooled_ref, *refs):
    pieces, out_ref = refs[:heads], refs[heads]
    q = pooled_ref[...].astype(F32)
    lane = lax.broadcasted_iota(jnp.int32, (heads, heads), 1)
    logits = jnp.zeros((heads, heads), F32)
    for d in range(heads):
        one = jnp.sum(q * pieces[d][...].astype(F32), axis=1, keepdims=True)
        logits = jnp.where(lane == (me_ref[0] ^ d), one / math.sqrt(DH), logits)
    out_ref[...] = logits


def logits_of(me, pooled_q, pieces):
    heads = len(pieces)
    rows = pl.BlockSpec((heads, DH), lambda i, m: (BS // heads, 0))
    return pl.pallas_call(
        functools.partial(logits_kernel, heads),
        grid_spec=pltpu.PrefetchScalarGridSpec(
            num_scalar_prefetch=1,
            grid=(1,),
            in_specs=[pl.BlockSpec((heads, DH), lambda i, m: (0, 0))] + [rows] * heads,
            out_specs=pl.BlockSpec((heads, heads), lambda i, m: (0, 0)),
        ),
        out_shape=jax.ShapeDtypeStruct((heads, heads), F32),
    )(me, pooled_q, *pieces)


def attend_kernel(me_ref, q_ref, tile_ref, k_ref, v_ref, *refs):
    packed, (out_ref, far_ref, sem) = refs[:-3], refs[-3:]
    source = me_ref[0] ^ jnp.max(tile_ref[...].astype(F32)).astype(jnp.int32)
    copies = [pltpu.make_async_copy(one, far_ref, sem) for one in packed]
    for n, copy in enumerate(copies):
        pl.when(source == n)(copy.start)
    q = q_ref[...]

    def part(keys, values):
        s = lax.dot_general(q, keys, (((1,), (1,)), ((), ())), preferred_element_type=F32)
        top = jnp.max(s, axis=1, keepdims=True) * SCALE
        w = jnp.exp2(s * SCALE - top).astype(BF16)
        total = jnp.sum(w.astype(F32), axis=1, keepdims=True)
        return top, total, jnp.dot(w, values, preferred_element_type=F32)

    own_max, own_total, own_sum = part(k_ref[...], v_ref[...])
    copies[0].wait()
    far_max, far_total, far_sum = part(far_ref[pl.ds(0, BS), :], far_ref[pl.ds(BS, BS), :])
    joint = jnp.maximum(own_max, far_max)
    own_e = jnp.exp2(own_max - joint)
    far_e = jnp.exp2(far_max - joint)
    inverse = 1.0 / (own_e * own_total + far_e * far_total)
    out_ref[...] = ((own_e * inverse) * own_sum + (far_e * inverse) * far_sum).astype(BF16)


def attend(me, d, q, packed):
    def rows(n):
        return pl.BlockSpec((BS, DH), lambda i, m: (n, 0))

    return pl.pallas_call(
        attend_kernel,
        grid_spec=pltpu.PrefetchScalarGridSpec(
            num_scalar_prefetch=1,
            grid=(1,),
            in_specs=[
                rows(0),
                pl.BlockSpec((TILE, DH), lambda i, m: (q.shape[0] // TILE - 1, 0)),
                rows(0),
                rows(1),
            ]
            + [pl.BlockSpec(memory_space=pl.ANY)] * len(packed),
            out_specs=rows(0),
            scratch_shapes=[pltpu.VMEM((2 * BS, DH), BF16), pltpu.SemaphoreType.DMA],
        ),
        out_shape=jax.ShapeDtypeStruct((BS, DH), BF16),
        compiler_params=pltpu.CompilerParams(vmem_limit_bytes=16 << 20),
        cost_estimate=pl.CostEstimate(
            flops=8 * BS * BS * DH, transcendentals=2 * BS * BS, bytes_accessed=12 * BS * DH
        ),
    )(me, q, q, packed[d], packed[d], *packed)


def join_kernel(members, me_ref, *refs):
    pieces, out_ref = refs[:members], refs[members]
    for d in range(members):
        first = pl.multiple_of((me_ref[0] ^ d) * DH, DH)
        out_ref[:, pl.ds(first, DH)] = pieces[d][...]


def join_heads(me, pieces):
    members = len(pieces)
    tok = pieces[0].shape[0]
    piece = pl.BlockSpec((tok, DH), lambda i, m: (0, 0))
    return pl.pallas_call(
        functools.partial(join_kernel, members),
        grid_spec=pltpu.PrefetchScalarGridSpec(
            num_scalar_prefetch=1,
            grid=(1,),
            in_specs=[piece] * members,
            out_specs=pl.BlockSpec((tok, members * DH), lambda i, m: (0, 0)),
        ),
        out_shape=jax.ShapeDtypeStruct((tok, members * DH), BF16),
        compiler_params=pltpu.CompilerParams(vmem_limit_bytes=16 << 20),
        cost_estimate=pl.CostEstimate(
            flops=0, transcendentals=0, bytes_accessed=4 * members * tok * DH
        ),
    )(me, *pieces)


def after(x, *earlier):
    return lax.optimization_barrier((x, *earlier))[0]


def by_heads(query_rows, key_rows, value_rows, selection):
    members = lax.axis_size("context")
    me = lax.axis_index("context")
    tok, width = query_rows.shape
    heads = width // DH
    here = me.astype(jnp.int32)[None]
    near = list(range(1, members // 2))
    far = list(range(members // 2, members))[::-1]

    def send(x, d):
        return lax.ppermute(x, "context", [(i, i ^ d) for i in range(members)])

    packed = [pack_head(here, d, key_rows, value_rows) for d in range(members)]
    got = {}

    def exchange(pieces, kind, ds, window, done):
        for d in ds:
            earlier = [got[done[-window]]] if len(done) >= window else []
            got[kind, d] = send(after(pieces[d], *earlier), d)
            done.append((kind, d))

    far_done, near_done = [], []
    exchange(packed, 0, far[::-1], 3, far_done)
    exchange(packed, 0, near, 2, near_done)
    chosen = jnp.broadcast_to(selection.astype(BF16)[:, :, None], (heads, TILE, DH))
    pooled_q, *pieces = cut_queries(
        here, after(query_rows, got[0, members // 2]), key_rows, chosen
    )
    exchange(pieces, 1, near, 2, near_done)
    exchange(pieces, 1, far[::-1], 3, far_done)
    packed = packed[:1] + [got[0, d] for d in range(1, members)]
    queries = pieces[:1] + [got[1, d] for d in range(1, members)]
    sort_logits = logits_of(here, pooled_q, queries)

    outputs = [None] * members
    for d in far[::-1] + near + [0]:
        outputs[d] = attend(here, d, queries[d], packed)
        if d:
            outputs[d] = send(outputs[d], d)
    attended = join_heads(here, outputs)
    return attended, sort_logits.reshape(heads, 1, members)


def solution(mesh):
    members = mesh.shape["context"]

    def per_device(query_rows, key_rows, value_rows, selection):
        tok, width = query_rows.shape
        fits = tok == BS and width == members * DH and members & (members - 1) == 0
        if fits and members == TILE:
            return by_heads(query_rows, key_rows, value_rows, selection)
        return any_size(query_rows, key_rows, value_rows, selection)

    placed = (
        P(("groups", "context"), "tensor"),
        P(("groups", "context"), "tensor"),
        P(("groups", "context"), "tensor"),
        P("tensor", ("groups", "context")),
    )
    return jax.shard_map(
        per_device,
        mesh=mesh,
        in_specs=placed,
        out_specs=(P(("groups", "context"), "tensor"), P("tensor", ("groups", "context"), None)),
        check_vma=False,
    )
```

```python
import functools
import math

import jax
import jax.numpy as jnp
from jax import lax
from jax.experimental import pallas as pl
from jax.experimental.pallas import tpu as pltpu
from jax.sharding import PartitionSpec as P

DH = 128
BS = 512
BF16 = jnp.bfloat16
F32 = jnp.float32


def block_partial(query_block, key_block, value_block):
    scores = jnp.dot(query_block, key_block.T, preferred_element_type=jnp.float32) * (
        1.0 / math.sqrt(DH)
    )
    row_max = jnp.max(scores, axis=1, keepdims=True)
    weights = jnp.exp(scores - row_max).astype(jnp.bfloat16)
    row_total = jnp.sum(weights.astype(jnp.float32), axis=1, keepdims=True)
    partial_sum = jnp.dot(weights, value_block, preferred_element_type=jnp.float32)
    return (row_max, row_total, partial_sum)


def combine_parts(own_part, far_part):
    own_max, own_total, own_sum = own_part
    far_max, far_total, far_sum = far_part
    joint = jnp.maximum(own_max, far_max)
    own_factor = jnp.exp(own_max - joint)
    far_factor = jnp.exp(far_max - joint)
    merged = (own_factor * own_sum + far_factor * far_sum) / (
        own_factor * own_total + far_factor * far_total
    )
    return merged.astype(jnp.bfloat16)


def any_size(query_rows, key_rows, value_rows, selection):
    members = lax.axis_size("context")
    tok_rows, width = query_rows.shape
    blocks = tok_rows // BS
    head_count = width // DH
    piece_rows = BS // members

    def pooled(rows_in):
        sums = jnp.sum(rows_in.reshape(blocks, BS, width), axis=1, dtype=jnp.float32) / math.sqrt(
            BS
        )
        return sums.astype(jnp.bfloat16).reshape(blocks, head_count, DH).transpose(1, 0, 2)

    pooled_q = pooled(query_rows)
    pooled_k = pooled(key_rows)
    products = jnp.einsum(
        "hbd,hcd->hbc",
        pooled_q,
        lax.all_gather(pooled_k, "context", axis=1, tiled=True),
        preferred_element_type=jnp.float32,
    )
    sort_logits = products / math.sqrt(DH)
    wanted = lax.all_gather(selection, "context", axis=1, tiled=True)
    query_grid = query_rows.reshape(blocks, BS, head_count, DH)
    key_grid = key_rows.reshape(blocks, BS, head_count, DH)
    value_grid = value_rows.reshape(blocks, BS, head_count, DH)
    pair_ids = jnp.arange(blocks * head_count, dtype=jnp.int32)

    def slice_pair(array, block, head):
        return lax.dynamic_slice(array, (block, 0, head, 0), (1, BS, 1, DH)).reshape(BS, DH)

    def pick_rows(held, table):
        inner = held.shape[-1] // head_count
        order_ids = table.reshape(head_count, members, blocks).transpose(2, 1, 0)
        source_dev = (order_ids // blocks)[:, :, None, :]
        source_blk = (order_ids % blocks)[:, :, None, :]
        row_ids = jnp.arange(piece_rows)[None, None, :, None]
        head_ids = jnp.arange(head_count)[None, None, None, :]
        grid = held.reshape(blocks, members, piece_rows, head_count, inner)
        return grid[source_blk, source_dev, row_ids, head_ids].reshape(
            blocks, members, piece_rows, head_count * inner
        )

    spread_k = key_rows.reshape(blocks, members, piece_rows, width)
    spread_v = value_rows.reshape(blocks, members, piece_rows, width)
    held_k = lax.all_to_all(spread_k, "context", split_axis=1, concat_axis=1, tiled=True)
    held_v = lax.all_to_all(spread_v, "context", split_axis=1, concat_axis=1, tiled=True)
    far_k = lax.all_to_all(
        pick_rows(held_k, wanted), "context", split_axis=1, concat_axis=1, tiled=True
    )
    far_v = lax.all_to_all(
        pick_rows(held_v, wanted), "context", split_axis=1, concat_axis=1, tiled=True
    )
    far_keys = far_k.reshape(blocks, BS, head_count, DH)
    far_values = far_v.reshape(blocks, BS, head_count, DH)

    def both_pair(pair_index):
        block = pair_index // head_count
        head = pair_index % head_count
        query_block = slice_pair(query_grid, block, head)
        own = block_partial(
            query_block, slice_pair(key_grid, block, head), slice_pair(value_grid, block, head)
        )
        far = block_partial(
            query_block, slice_pair(far_keys, block, head), slice_pair(far_values, block, head)
        )
        return combine_parts(own, far)

    outputs = lax.map(both_pair, pair_ids)
    attended = (
        outputs.reshape(blocks, head_count, BS, DH).transpose(0, 2, 1, 3).reshape(tok_rows, width)
    )
    return (attended, sort_logits)


SCALE = math.log2(math.e) / math.sqrt(DH)
TILE = 8


def pack_kernel(me_ref, k_ref, v_ref, out_ref):
    out_ref[pl.ds(0, BS), :] = k_ref[...]
    out_ref[pl.ds(BS, BS), :] = v_ref[...]


def pack_head(me, d, k, v):
    rows = 2 * BS
    part = pl.BlockSpec((BS, DH), lambda i, m: (0, m[0] ^ d))
    return pl.pallas_call(
        pack_kernel,
        grid_spec=pltpu.PrefetchScalarGridSpec(
            num_scalar_prefetch=1,
            grid=(1,),
            in_specs=[part, part],
            out_specs=pl.BlockSpec((rows, DH), lambda i, m: (0, 0)),
        ),
        out_shape=jax.ShapeDtypeStruct((rows, DH), BF16),
        cost_estimate=pl.CostEstimate(
            flops=0, transcendentals=0, bytes_accessed=4 * rows * DH
        ),
    )(me, k, v)


def pooled(array):
    return (jnp.sum(array.astype(F32), axis=0, keepdims=True) / math.sqrt(BS)).astype(BF16)


def cut_kernel(heads, me_ref, q_ref, k_ref, chosen_ref, pooled_ref, *pieces):
    def by_head(row):
        return jnp.concatenate([row[:, h * DH : (h + 1) * DH] for h in range(heads)], axis=0)

    pooled_ref[...] = by_head(pooled(q_ref[...]))
    pooled_keys = by_head(pooled(k_ref[...]))
    for d in range(heads):
        first = pl.multiple_of((me_ref[0] ^ d) * DH, DH)
        pieces[d][pl.ds(0, BS), :] = q_ref[:, pl.ds(first, DH)]
        pieces[d][pl.ds(BS, heads), :] = pooled_keys
        pieces[d][pl.ds(BS + heads, TILE), :] = chosen_ref[me_ref[0] ^ d]


def cut_queries(me, q, k, chosen):
    tok, width = q.shape
    heads = width // DH
    whole = pl.BlockSpec((tok, width), lambda i, m: (0, 0))
    piece = pl.BlockSpec((tok + heads + TILE, DH), lambda i, m: (0, 0))
    return pl.pallas_call(
        functools.partial(cut_kernel, heads),
        grid_spec=pltpu.PrefetchScalarGridSpec(
            num_scalar_prefetch=1,
            grid=(1,),
            in_specs=[whole, whole, pl.BlockSpec((heads, TILE, DH), lambda i, m: (0, 0, 0))],
            out_specs=[pl.BlockSpec((heads, DH), lambda i, m: (0, 0))] + [piece] * heads,
        ),
        out_shape=[jax.ShapeDtypeStruct((heads, DH), BF16)]
        + [jax.ShapeDtypeStruct((tok + heads + TILE, DH), BF16)] * heads,
        compiler_params=pltpu.CompilerParams(vmem_limit_bytes=24 << 20),
        cost_estimate=pl.CostEstimate(
            flops=2 * tok * width, transcendentals=0, bytes_accessed=6 * tok * width
        ),
    )(me, q, k, chosen)


def logits_kernel(heads, me_ref, pooled_ref, *refs):
    pieces, out_ref = refs[:heads], refs[heads]
    q = pooled_ref[...].astype(F32)
    lane = lax.broadcasted_iota(jnp.int32, (heads, heads), 1)
    logits = jnp.zeros((heads, heads), F32)
    for d in range(heads):
        one = jnp.sum(q * pieces[d][...].astype(F32), axis=1, keepdims=True)
        logits = jnp.where(lane == (me_ref[0] ^ d), one / math.sqrt(DH), logits)
    out_ref[...] = logits


def logits_of(me, pooled_q, pieces):
    heads = len(pieces)
    rows = pl.BlockSpec((heads, DH), lambda i, m: (BS // heads, 0))
    return pl.pallas_call(
        functools.partial(logits_kernel, heads),
        grid_spec=pltpu.PrefetchScalarGridSpec(
            num_scalar_prefetch=1,
            grid=(1,),
            in_specs=[pl.BlockSpec((heads, DH), lambda i, m: (0, 0))] + [rows] * heads,
            out_specs=pl.BlockSpec((heads, heads), lambda i, m: (0, 0)),
        ),
        out_shape=jax.ShapeDtypeStruct((heads, heads), F32),
    )(me, pooled_q, *pieces)


def attend_kernel(me_ref, q_ref, tile_ref, k_ref, v_ref, *refs):
    packed, (out_ref, far_ref, sem) = refs[:-3], refs[-3:]
    source = me_ref[0] ^ jnp.max(tile_ref[...].astype(F32)).astype(jnp.int32)
    copies = [pltpu.make_async_copy(one, far_ref, sem) for one in packed]
    for n, copy in enumerate(copies):
        pl.when(source == n)(copy.start)
    q = q_ref[...]

    def part(keys, values):
        s = lax.dot_general(q, keys, (((1,), (1,)), ((), ())), preferred_element_type=F32)
        top = jnp.max(s, axis=1, keepdims=True) * SCALE
        w = jnp.exp2(s * SCALE - top).astype(BF16)
        total = jnp.sum(w.astype(F32), axis=1, keepdims=True)
        return top, total, jnp.dot(w, values, preferred_element_type=F32)

    own_max, own_total, own_sum = part(k_ref[...], v_ref[...])
    copies[0].wait()
    far_max, far_total, far_sum = part(far_ref[pl.ds(0, BS), :], far_ref[pl.ds(BS, BS), :])
    joint = jnp.maximum(own_max, far_max)
    own_e = jnp.exp2(own_max - joint)
    far_e = jnp.exp2(far_max - joint)
    inverse = 1.0 / (own_e * own_total + far_e * far_total)
    out_ref[...] = ((own_e * inverse) * own_sum + (far_e * inverse) * far_sum).astype(BF16)


def attend(me, d, q, packed):
    def rows(n):
        return pl.BlockSpec((BS, DH), lambda i, m: (n, 0))

    return pl.pallas_call(
        attend_kernel,
        grid_spec=pltpu.PrefetchScalarGridSpec(
            num_scalar_prefetch=1,
            grid=(1,),
            in_specs=[
                rows(0),
                pl.BlockSpec((TILE, DH), lambda i, m: (q.shape[0] // TILE - 1, 0)),
                rows(0),
                rows(1),
            ]
            + [pl.BlockSpec(memory_space=pl.ANY)] * len(packed),
            out_specs=rows(0),
            scratch_shapes=[pltpu.VMEM((2 * BS, DH), BF16), pltpu.SemaphoreType.DMA],
        ),
        out_shape=jax.ShapeDtypeStruct((BS, DH), BF16),
        compiler_params=pltpu.CompilerParams(vmem_limit_bytes=16 << 20),
        cost_estimate=pl.CostEstimate(
            flops=8 * BS * BS * DH, transcendentals=2 * BS * BS, bytes_accessed=12 * BS * DH
        ),
    )(me, q, q, packed[d], packed[d], *packed)


def join_kernel(members, me_ref, *refs):
    pieces, out_ref = refs[:members], refs[members]
    for d in range(members):
        first = pl.multiple_of((me_ref[0] ^ d) * DH, DH)
        out_ref[:, pl.ds(first, DH)] = pieces[d][...]


def join_heads(me, pieces):
    members = len(pieces)
    tok = pieces[0].shape[0]
    piece = pl.BlockSpec((tok, DH), lambda i, m: (0, 0))
    return pl.pallas_call(
        functools.partial(join_kernel, members),
        grid_spec=pltpu.PrefetchScalarGridSpec(
            num_scalar_prefetch=1,
            grid=(1,),
            in_specs=[piece] * members,
            out_specs=pl.BlockSpec((tok, members * DH), lambda i, m: (0, 0)),
        ),
        out_shape=jax.ShapeDtypeStruct((tok, members * DH), BF16),
        compiler_params=pltpu.CompilerParams(vmem_limit_bytes=16 << 20),
        cost_estimate=pl.CostEstimate(
            flops=0, transcendentals=0, bytes_accessed=4 * members * tok * DH
        ),
    )(me, *pieces)


def after(x, *earlier):
    return lax.optimization_barrier((x, *earlier))[0]


def by_heads(query_rows, key_rows, value_rows, selection):
    members = lax.axis_size("context")
    me = lax.axis_index("context")
    tok, width = query_rows.shape
    heads = width // DH
    here = me.astype(jnp.int32)[None]
    near = list(range(1, members // 2))
    far = list(range(members // 2, members))[::-1]

    def send(x, d):
        return lax.ppermute(x, "context", [(i, i ^ d) for i in range(members)])

    packed = [pack_head(here, d, key_rows, value_rows) for d in range(members)]
    got = {}

    def exchange(pieces, kind, ds, window, done):
        for d in ds:
            earlier = [got[done[-window]]] if len(done) >= window else []
            got[kind, d] = send(after(pieces[d], *earlier), d)
            done.append((kind, d))

    far_done, near_done = [], []
    exchange(packed, 0, far[::-1], 3, far_done)
    exchange(packed, 0, near, 2, near_done)
    chosen = jnp.broadcast_to(selection.astype(BF16)[:, :, None], (heads, TILE, DH))
    pooled_q, *pieces = cut_queries(
        here, after(query_rows, got[0, members // 2], packed[0]), key_rows, chosen
    )
    exchange(pieces, 1, near, 2, near_done)
    exchange(pieces, 1, far[::-1], 3, far_done)
    packed = packed[:1] + [got[0, d] for d in range(1, members)]
    queries = pieces[:1] + [got[1, d] for d in range(1, members)]
    sort_logits = logits_of(here, pooled_q, queries)

    outputs = [None] * members
    for d in far[::-1] + near + [0]:
        outputs[d] = attend(here, d, queries[d], packed)
        if d:
            outputs[d] = send(outputs[d], d)
    attended = join_heads(here, outputs)
    return attended, sort_logits.reshape(heads, 1, members)


def solution(mesh):
    members = mesh.shape["context"]

    def per_device(query_rows, key_rows, value_rows, selection):
        tok, width = query_rows.shape
        fits = tok == BS and width == members * DH and members & (members - 1) == 0
        if fits and members == TILE:
            return by_heads(query_rows, key_rows, value_rows, selection)
        return any_size(query_rows, key_rows, value_rows, selection)

    placed = (
        P(("groups", "context"), "tensor"),
        P(("groups", "context"), "tensor"),
        P(("groups", "context"), "tensor"),
        P("tensor", ("groups", "context")),
    )
    return jax.shard_map(
        per_device,
        mesh=mesh,
        in_specs=placed,
        out_specs=(P(("groups", "context"), "tensor"), P("tensor", ("groups", "context"), None)),
        check_vma=False,
    )
```

```python
import functools
import math

import jax
import jax.numpy as jnp
from jax import lax
from jax.experimental import pallas as pl
from jax.experimental.pallas import tpu as pltpu
from jax.sharding import PartitionSpec as P

DH = 128
BS = 512
BF16 = jnp.bfloat16
F32 = jnp.float32


def block_partial(query_block, key_block, value_block):
    scores = jnp.dot(query_block, key_block.T, preferred_element_type=jnp.float32) * (
        1.0 / math.sqrt(DH)
    )
    row_max = jnp.max(scores, axis=1, keepdims=True)
    weights = jnp.exp(scores - row_max).astype(jnp.bfloat16)
    row_total = jnp.sum(weights.astype(jnp.float32), axis=1, keepdims=True)
    partial_sum = jnp.dot(weights, value_block, preferred_element_type=jnp.float32)
    return (row_max, row_total, partial_sum)


def combine_parts(own_part, far_part):
    own_max, own_total, own_sum = own_part
    far_max, far_total, far_sum = far_part
    joint = jnp.maximum(own_max, far_max)
    own_factor = jnp.exp(own_max - joint)
    far_factor = jnp.exp(far_max - joint)
    merged = (own_factor * own_sum + far_factor * far_sum) / (
        own_factor * own_total + far_factor * far_total
    )
    return merged.astype(jnp.bfloat16)


def any_size(query_rows, key_rows, value_rows, selection):
    members = lax.axis_size("context")
    tok_rows, width = query_rows.shape
    blocks = tok_rows // BS
    head_count = width // DH
    piece_rows = BS // members

    def pooled(rows_in):
        sums = jnp.sum(rows_in.reshape(blocks, BS, width), axis=1, dtype=jnp.float32) / math.sqrt(
            BS
        )
        return sums.astype(jnp.bfloat16).reshape(blocks, head_count, DH).transpose(1, 0, 2)

    pooled_q = pooled(query_rows)
    pooled_k = pooled(key_rows)
    products = jnp.einsum(
        "hbd,hcd->hbc",
        pooled_q,
        lax.all_gather(pooled_k, "context", axis=1, tiled=True),
        preferred_element_type=jnp.float32,
    )
    sort_logits = products / math.sqrt(DH)
    wanted = lax.all_gather(selection, "context", axis=1, tiled=True)
    query_grid = query_rows.reshape(blocks, BS, head_count, DH)
    key_grid = key_rows.reshape(blocks, BS, head_count, DH)
    value_grid = value_rows.reshape(blocks, BS, head_count, DH)
    pair_ids = jnp.arange(blocks * head_count, dtype=jnp.int32)

    def slice_pair(array, block, head):
        return lax.dynamic_slice(array, (block, 0, head, 0), (1, BS, 1, DH)).reshape(BS, DH)

    def pick_rows(held, table):
        inner = held.shape[-1] // head_count
        order_ids = table.reshape(head_count, members, blocks).transpose(2, 1, 0)
        source_dev = (order_ids // blocks)[:, :, None, :]
        source_blk = (order_ids % blocks)[:, :, None, :]
        row_ids = jnp.arange(piece_rows)[None, None, :, None]
        head_ids = jnp.arange(head_count)[None, None, None, :]
        grid = held.reshape(blocks, members, piece_rows, head_count, inner)
        return grid[source_blk, source_dev, row_ids, head_ids].reshape(
            blocks, members, piece_rows, head_count * inner
        )

    spread_k = key_rows.reshape(blocks, members, piece_rows, width)
    spread_v = value_rows.reshape(blocks, members, piece_rows, width)
    held_k = lax.all_to_all(spread_k, "context", split_axis=1, concat_axis=1, tiled=True)
    held_v = lax.all_to_all(spread_v, "context", split_axis=1, concat_axis=1, tiled=True)
    far_k = lax.all_to_all(
        pick_rows(held_k, wanted), "context", split_axis=1, concat_axis=1, tiled=True
    )
    far_v = lax.all_to_all(
        pick_rows(held_v, wanted), "context", split_axis=1, concat_axis=1, tiled=True
    )
    far_keys = far_k.reshape(blocks, BS, head_count, DH)
    far_values = far_v.reshape(blocks, BS, head_count, DH)

    def both_pair(pair_index):
        block = pair_index // head_count
        head = pair_index % head_count
        query_block = slice_pair(query_grid, block, head)
        own = block_partial(
            query_block, slice_pair(key_grid, block, head), slice_pair(value_grid, block, head)
        )
        far = block_partial(
            query_block, slice_pair(far_keys, block, head), slice_pair(far_values, block, head)
        )
        return combine_parts(own, far)

    outputs = lax.map(both_pair, pair_ids)
    attended = (
        outputs.reshape(blocks, head_count, BS, DH).transpose(0, 2, 1, 3).reshape(tok_rows, width)
    )
    return (attended, sort_logits)


SCALE = math.log2(math.e) / math.sqrt(DH)
TILE = 8


def pack_kernel(me_ref, k_ref, v_ref, out_ref):
    out_ref[pl.ds(0, BS), :] = k_ref[...]
    out_ref[pl.ds(BS, BS), :] = v_ref[...]


def pack_head(me, d, k, v):
    rows = 2 * BS
    part = pl.BlockSpec((BS, DH), lambda i, m: (0, m[0] ^ d))
    return pl.pallas_call(
        pack_kernel,
        grid_spec=pltpu.PrefetchScalarGridSpec(
            num_scalar_prefetch=1,
            grid=(1,),
            in_specs=[part, part],
            out_specs=pl.BlockSpec((rows, DH), lambda i, m: (0, 0)),
        ),
        out_shape=jax.ShapeDtypeStruct((rows, DH), BF16),
        cost_estimate=pl.CostEstimate(
            flops=0, transcendentals=0, bytes_accessed=4 * rows * DH
        ),
    )(me, k, v)


def pooled(array):
    return (jnp.sum(array.astype(F32), axis=0, keepdims=True) / math.sqrt(BS)).astype(BF16)


def cut_kernel(heads, me_ref, q_ref, k_ref, chosen_ref, pooled_ref, *pieces):
    def by_head(row):
        return jnp.concatenate([row[:, h * DH : (h + 1) * DH] for h in range(heads)], axis=0)

    pooled_ref[...] = by_head(pooled(q_ref[...]))
    pooled_keys = by_head(pooled(k_ref[...]))
    for d in range(heads):
        first = pl.multiple_of((me_ref[0] ^ d) * DH, DH)
        pieces[d][pl.ds(0, BS), :] = q_ref[:, pl.ds(first, DH)]
        pieces[d][pl.ds(BS, heads), :] = pooled_keys
        pieces[d][pl.ds(BS + heads, TILE), :] = chosen_ref[me_ref[0] ^ d]


def cut_queries(me, q, k, chosen):
    tok, width = q.shape
    heads = width // DH
    whole = pl.BlockSpec((tok, width), lambda i, m: (0, 0))
    piece = pl.BlockSpec((tok + heads + TILE, DH), lambda i, m: (0, 0))
    return pl.pallas_call(
        functools.partial(cut_kernel, heads),
        grid_spec=pltpu.PrefetchScalarGridSpec(
            num_scalar_prefetch=1,
            grid=(1,),
            in_specs=[whole, whole, pl.BlockSpec((heads, TILE, DH), lambda i, m: (0, 0, 0))],
            out_specs=[pl.BlockSpec((heads, DH), lambda i, m: (0, 0))] + [piece] * heads,
        ),
        out_shape=[jax.ShapeDtypeStruct((heads, DH), BF16)]
        + [jax.ShapeDtypeStruct((tok + heads + TILE, DH), BF16)] * heads,
        compiler_params=pltpu.CompilerParams(vmem_limit_bytes=24 << 20),
        cost_estimate=pl.CostEstimate(
            flops=2 * tok * width, transcendentals=0, bytes_accessed=6 * tok * width
        ),
    )(me, q, k, chosen)


def logits_kernel(heads, me_ref, pooled_ref, *refs):
    pieces, out_ref = refs[:heads], refs[heads]
    q = pooled_ref[...].astype(F32)
    lane = lax.broadcasted_iota(jnp.int32, (heads, heads), 1)
    logits = jnp.zeros((heads, heads), F32)
    for d in range(heads):
        one = jnp.sum(q * pieces[d][...].astype(F32), axis=1, keepdims=True)
        logits = jnp.where(lane == (me_ref[0] ^ d), one / math.sqrt(DH), logits)
    out_ref[...] = logits


def logits_of(me, pooled_q, pieces):
    heads = len(pieces)
    rows = pl.BlockSpec((heads, DH), lambda i, m: (BS // heads, 0))
    return pl.pallas_call(
        functools.partial(logits_kernel, heads),
        grid_spec=pltpu.PrefetchScalarGridSpec(
            num_scalar_prefetch=1,
            grid=(1,),
            in_specs=[pl.BlockSpec((heads, DH), lambda i, m: (0, 0))] + [rows] * heads,
            out_specs=pl.BlockSpec((heads, heads), lambda i, m: (0, 0)),
        ),
        out_shape=jax.ShapeDtypeStruct((heads, heads), F32),
    )(me, pooled_q, *pieces)


def attend_kernel(me_ref, q_ref, tile_ref, k_ref, v_ref, *refs):
    packed, (out_ref, far_ref, sem) = refs[:-3], refs[-3:]
    source = me_ref[0] ^ jnp.max(tile_ref[...].astype(F32)).astype(jnp.int32)
    copies = [pltpu.make_async_copy(one, far_ref, sem) for one in packed]
    for n, copy in enumerate(copies):
        pl.when(source == n)(copy.start)
    q = q_ref[...]

    def part(keys, values):
        s = lax.dot_general(q, keys, (((1,), (1,)), ((), ())), preferred_element_type=F32)
        top = jnp.max(s, axis=1, keepdims=True) * SCALE
        w = jnp.exp2(s * SCALE - top).astype(BF16)
        total = jnp.sum(w.astype(F32), axis=1, keepdims=True)
        return top, total, jnp.dot(w, values, preferred_element_type=F32)

    own_max, own_total, own_sum = part(k_ref[...], v_ref[...])
    copies[0].wait()
    far_max, far_total, far_sum = part(far_ref[pl.ds(0, BS), :], far_ref[pl.ds(BS, BS), :])
    joint = jnp.maximum(own_max, far_max)
    own_e = jnp.exp2(own_max - joint)
    far_e = jnp.exp2(far_max - joint)
    inverse = 1.0 / (own_e * own_total + far_e * far_total)
    out_ref[...] = ((own_e * inverse) * own_sum + (far_e * inverse) * far_sum).astype(BF16)


def attend(me, d, q, packed):
    def rows(n):
        return pl.BlockSpec((BS, DH), lambda i, m: (n, 0))

    return pl.pallas_call(
        attend_kernel,
        grid_spec=pltpu.PrefetchScalarGridSpec(
            num_scalar_prefetch=1,
            grid=(1,),
            in_specs=[
                rows(0),
                pl.BlockSpec((TILE, DH), lambda i, m: (q.shape[0] // TILE - 1, 0)),
                rows(0),
                rows(1),
            ]
            + [pl.BlockSpec(memory_space=pl.ANY)] * len(packed),
            out_specs=rows(0),
            scratch_shapes=[pltpu.VMEM((2 * BS, DH), BF16), pltpu.SemaphoreType.DMA],
        ),
        out_shape=jax.ShapeDtypeStruct((BS, DH), BF16),
        compiler_params=pltpu.CompilerParams(vmem_limit_bytes=16 << 20),
        cost_estimate=pl.CostEstimate(
            flops=8 * BS * BS * DH, transcendentals=2 * BS * BS, bytes_accessed=12 * BS * DH
        ),
    )(me, q, q, packed[d], packed[d], *packed)


def join_kernel(members, me_ref, *refs):
    pieces, out_ref = refs[:members], refs[members]
    for d in range(members):
        first = pl.multiple_of((me_ref[0] ^ d) * DH, DH)
        out_ref[:, pl.ds(first, DH)] = pieces[d][...]


def join_heads(me, pieces):
    members = len(pieces)
    tok = pieces[0].shape[0]
    piece = pl.BlockSpec((tok, DH), lambda i, m: (0, 0))
    return pl.pallas_call(
        functools.partial(join_kernel, members),
        grid_spec=pltpu.PrefetchScalarGridSpec(
            num_scalar_prefetch=1,
            grid=(1,),
            in_specs=[piece] * members,
            out_specs=pl.BlockSpec((tok, members * DH), lambda i, m: (0, 0)),
        ),
        out_shape=jax.ShapeDtypeStruct((tok, members * DH), BF16),
        compiler_params=pltpu.CompilerParams(vmem_limit_bytes=16 << 20),
        cost_estimate=pl.CostEstimate(
            flops=0, transcendentals=0, bytes_accessed=4 * members * tok * DH
        ),
    )(me, *pieces)


def after(x, *earlier):
    return lax.optimization_barrier((x, *earlier))[0]


def by_heads(query_rows, key_rows, value_rows, selection):
    members = lax.axis_size("context")
    me = lax.axis_index("context")
    tok, width = query_rows.shape
    heads = width // DH
    here = me.astype(jnp.int32)[None]
    near = list(range(1, members // 2))
    far = list(range(members // 2, members))[::-1]

    def send(x, d):
        return lax.ppermute(x, "context", [(i, i ^ d) for i in range(members)])

    packed = [pack_head(here, d, key_rows, value_rows) for d in range(members)]
    got = {}

    def exchange(pieces, kind, ds, window, done):
        for d in ds:
            earlier = [got[done[-window]]] if len(done) >= window else []
            got[kind, d] = send(after(pieces[d], *earlier), d)
            done.append((kind, d))

    far_done, near_done = [], []
    exchange(packed, 0, far[::-1], 3, far_done)
    exchange(packed, 0, near, 2, near_done)
    chosen = jnp.broadcast_to(selection.astype(BF16)[:, :, None], (heads, TILE, DH))
    pooled_q, *pieces = cut_queries(
        here, after(query_rows, got[0, members // 2], packed[0]), key_rows, chosen
    )
    exchange(pieces, 1, [2, 1, 3], 2, near_done)
    exchange(pieces, 1, far[::-1], 3, far_done)
    packed = packed[:1] + [got[0, d] for d in range(1, members)]
    queries = pieces[:1] + [got[1, d] for d in range(1, members)]
    sort_logits = logits_of(here, pooled_q, queries)

    outputs = [None] * members
    for d in [0] + far[::-1] + near:
        outputs[d] = attend(here, d, queries[d], packed)
        if d:
            outputs[d] = send(outputs[d], d)
    attended = join_heads(here, outputs)
    return attended, sort_logits.reshape(heads, 1, members)


def solution(mesh):
    members = mesh.shape["context"]

    def per_device(query_rows, key_rows, value_rows, selection):
        tok, width = query_rows.shape
        fits = tok == BS and width == members * DH and members & (members - 1) == 0
        if fits and members == TILE:
            return by_heads(query_rows, key_rows, value_rows, selection)
        return any_size(query_rows, key_rows, value_rows, selection)

    placed = (
        P(("groups", "context"), "tensor"),
        P(("groups", "context"), "tensor"),
        P(("groups", "context"), "tensor"),
        P("tensor", ("groups", "context")),
    )
    return jax.shard_map(
        per_device,
        mesh=mesh,
        in_specs=placed,
        out_specs=(P(("groups", "context"), "tensor"), P("tensor", ("groups", "context"), None)),
        check_vma=False,
    )
```

```python
import functools
import math

import jax
import jax.numpy as jnp
from jax import lax
from jax.experimental import pallas as pl
from jax.experimental.pallas import tpu as pltpu
from jax.sharding import PartitionSpec as P

DH = 128
BS = 512
BF16 = jnp.bfloat16
F32 = jnp.float32


def block_partial(query_block, key_block, value_block):
    scores = jnp.dot(query_block, key_block.T, preferred_element_type=jnp.float32) * (
        1.0 / math.sqrt(DH)
    )
    row_max = jnp.max(scores, axis=1, keepdims=True)
    weights = jnp.exp(scores - row_max).astype(jnp.bfloat16)
    row_total = jnp.sum(weights.astype(jnp.float32), axis=1, keepdims=True)
    partial_sum = jnp.dot(weights, value_block, preferred_element_type=jnp.float32)
    return (row_max, row_total, partial_sum)


def combine_parts(own_part, far_part):
    own_max, own_total, own_sum = own_part
    far_max, far_total, far_sum = far_part
    joint = jnp.maximum(own_max, far_max)
    own_factor = jnp.exp(own_max - joint)
    far_factor = jnp.exp(far_max - joint)
    merged = (own_factor * own_sum + far_factor * far_sum) / (
        own_factor * own_total + far_factor * far_total
    )
    return merged.astype(jnp.bfloat16)


def any_size(query_rows, key_rows, value_rows, selection):
    members = lax.axis_size("context")
    tok_rows, width = query_rows.shape
    blocks = tok_rows // BS
    head_count = width // DH
    piece_rows = BS // members

    def pooled(rows_in):
        sums = jnp.sum(rows_in.reshape(blocks, BS, width), axis=1, dtype=jnp.float32) / math.sqrt(
            BS
        )
        return sums.astype(jnp.bfloat16).reshape(blocks, head_count, DH).transpose(1, 0, 2)

    pooled_q = pooled(query_rows)
    pooled_k = pooled(key_rows)
    products = jnp.einsum(
        "hbd,hcd->hbc",
        pooled_q,
        lax.all_gather(pooled_k, "context", axis=1, tiled=True),
        preferred_element_type=jnp.float32,
    )
    sort_logits = products / math.sqrt(DH)
    wanted = lax.all_gather(selection, "context", axis=1, tiled=True)
    query_grid = query_rows.reshape(blocks, BS, head_count, DH)
    key_grid = key_rows.reshape(blocks, BS, head_count, DH)
    value_grid = value_rows.reshape(blocks, BS, head_count, DH)
    pair_ids = jnp.arange(blocks * head_count, dtype=jnp.int32)

    def slice_pair(array, block, head):
        return lax.dynamic_slice(array, (block, 0, head, 0), (1, BS, 1, DH)).reshape(BS, DH)

    def pick_rows(held, table):
        inner = held.shape[-1] // head_count
        order_ids = table.reshape(head_count, members, blocks).transpose(2, 1, 0)
        source_dev = (order_ids // blocks)[:, :, None, :]
        source_blk = (order_ids % blocks)[:, :, None, :]
        row_ids = jnp.arange(piece_rows)[None, None, :, None]
        head_ids = jnp.arange(head_count)[None, None, None, :]
        grid = held.reshape(blocks, members, piece_rows, head_count, inner)
        return grid[source_blk, source_dev, row_ids, head_ids].reshape(
            blocks, members, piece_rows, head_count * inner
        )

    spread_k = key_rows.reshape(blocks, members, piece_rows, width)
    spread_v = value_rows.reshape(blocks, members, piece_rows, width)
    held_k = lax.all_to_all(spread_k, "context", split_axis=1, concat_axis=1, tiled=True)
    held_v = lax.all_to_all(spread_v, "context", split_axis=1, concat_axis=1, tiled=True)
    far_k = lax.all_to_all(
        pick_rows(held_k, wanted), "context", split_axis=1, concat_axis=1, tiled=True
    )
    far_v = lax.all_to_all(
        pick_rows(held_v, wanted), "context", split_axis=1, concat_axis=1, tiled=True
    )
    far_keys = far_k.reshape(blocks, BS, head_count, DH)
    far_values = far_v.reshape(blocks, BS, head_count, DH)

    def both_pair(pair_index):
        block = pair_index // head_count
        head = pair_index % head_count
        query_block = slice_pair(query_grid, block, head)
        own = block_partial(
            query_block, slice_pair(key_grid, block, head), slice_pair(value_grid, block, head)
        )
        far = block_partial(
            query_block, slice_pair(far_keys, block, head), slice_pair(far_values, block, head)
        )
        return combine_parts(own, far)

    outputs = lax.map(both_pair, pair_ids)
    attended = (
        outputs.reshape(blocks, head_count, BS, DH).transpose(0, 2, 1, 3).reshape(tok_rows, width)
    )
    return (attended, sort_logits)


SCALE = math.log2(math.e) / math.sqrt(DH)
TILE = 8


def pack_kernel(me_ref, k_ref, v_ref, out_ref):
    out_ref[pl.ds(0, BS), :] = k_ref[...]
    out_ref[pl.ds(BS, BS), :] = v_ref[...]


def pack_head(me, d, k, v):
    rows = 2 * BS
    part = pl.BlockSpec((BS, DH), lambda i, m: (0, m[0] ^ d))
    return pl.pallas_call(
        pack_kernel,
        grid_spec=pltpu.PrefetchScalarGridSpec(
            num_scalar_prefetch=1,
            grid=(1,),
            in_specs=[part, part],
            out_specs=pl.BlockSpec((rows, DH), lambda i, m: (0, 0)),
        ),
        out_shape=jax.ShapeDtypeStruct((rows, DH), BF16),
        cost_estimate=pl.CostEstimate(
            flops=0, transcendentals=0, bytes_accessed=4 * rows * DH
        ),
    )(me, k, v)


def pooled(array):
    return (jnp.sum(array.astype(F32), axis=0, keepdims=True) / math.sqrt(BS)).astype(BF16)


def cut_kernel(heads, me_ref, q_ref, k_ref, chosen_ref, pooled_ref, *pieces):
    def by_head(row):
        return jnp.concatenate([row[:, h * DH : (h + 1) * DH] for h in range(heads)], axis=0)

    pooled_ref[...] = by_head(pooled(q_ref[...]))
    pooled_keys = by_head(pooled(k_ref[...]))
    for d in range(heads):
        first = pl.multiple_of((me_ref[0] ^ d) * DH, DH)
        pieces[d][pl.ds(0, BS), :] = q_ref[:, pl.ds(first, DH)]
        row = lax.broadcasted_iota(jnp.int32, pooled_keys.shape, 0)
        pieces[d][pl.ds(BS, heads), :] = jnp.where(
            row == (me_ref[0] ^ d),
            chosen_ref[me_ref[0] ^ d].astype(F32),
            pooled_keys.astype(F32),
        ).astype(BF16)


def cut_queries(me, q, k, chosen):
    tok, width = q.shape
    heads = width // DH
    whole = pl.BlockSpec((tok, width), lambda i, m: (0, 0))
    piece = pl.BlockSpec((tok + heads, DH), lambda i, m: (0, 0))
    return pl.pallas_call(
        functools.partial(cut_kernel, heads),
        grid_spec=pltpu.PrefetchScalarGridSpec(
            num_scalar_prefetch=1,
            grid=(1,),
            in_specs=[whole, whole, pl.BlockSpec((heads, TILE, DH), lambda i, m: (0, 0, 0))],
            out_specs=[pl.BlockSpec((heads, DH), lambda i, m: (0, 0))] + [piece] * heads,
        ),
        out_shape=[jax.ShapeDtypeStruct((heads, DH), BF16)]
        + [jax.ShapeDtypeStruct((tok + heads, DH), BF16)] * heads,
        compiler_params=pltpu.CompilerParams(vmem_limit_bytes=24 << 20),
        cost_estimate=pl.CostEstimate(
            flops=2 * tok * width, transcendentals=0, bytes_accessed=6 * tok * width
        ),
    )(me, q, k, chosen)


def logits_kernel(heads, me_ref, pooled_ref, *refs):
    pieces, keys, out_ref = refs[:heads], refs[heads:-1], refs[-1]
    row = lax.broadcasted_iota(jnp.int32, (heads, DH), 0)
    q = pooled_ref[...].astype(F32)
    lane = lax.broadcasted_iota(jnp.int32, (heads, heads), 1)
    logits = jnp.zeros((heads, heads), F32)
    for d in range(heads):
        rebuilt = keys[d][...].astype(F32)
        pooled_keys = jnp.where(row == me_ref[0], rebuilt, pieces[d][...].astype(F32))
        one = jnp.sum(q * pooled_keys, axis=1, keepdims=True)
        logits = jnp.where(lane == (me_ref[0] ^ d), one / math.sqrt(DH), logits)
    out_ref[...] = logits


def logits_of(me, pooled_q, pieces, packed):
    heads = len(pieces)
    rows = pl.BlockSpec((heads, DH), lambda i, m: (BS // heads, 0))
    return pl.pallas_call(
        functools.partial(logits_kernel, heads),
        grid_spec=pltpu.PrefetchScalarGridSpec(
            num_scalar_prefetch=1,
            grid=(1,),
            in_specs=[pl.BlockSpec((heads, DH), lambda i, m: (0, 0))]
            + [rows] * heads
            + [pl.BlockSpec((heads, DH), lambda i, m: (0, 0))] * heads,
            out_specs=pl.BlockSpec((heads, heads), lambda i, m: (0, 0)),
        ),
        out_shape=jax.ShapeDtypeStruct((heads, heads), F32),
    )(me, pooled_q, *pieces, *packed)


def attend_kernel(me_ref, q_ref, tile_ref, k_ref, v_ref, *refs):
    packed, (out_ref, pooled_ref, far_ref, sem) = refs[:-4], refs[-4:]
    row = lax.broadcasted_iota(jnp.int32, tile_ref.shape, 0)
    chosen = jnp.where(row == me_ref[0], tile_ref[...].astype(F32), -1.0)
    source = me_ref[0] ^ jnp.max(chosen).astype(jnp.int32)
    copies = [pltpu.make_async_copy(one, far_ref, sem) for one in packed]
    for n, copy in enumerate(copies):
        pl.when(source == n)(copy.start)
    q = q_ref[...]

    def part(keys, values):
        s = lax.dot_general(q, keys, (((1,), (1,)), ((), ())), preferred_element_type=F32)
        top = jnp.max(s, axis=1, keepdims=True) * SCALE
        w = jnp.exp2(s * SCALE - top).astype(BF16)
        total = jnp.sum(w.astype(F32), axis=1, keepdims=True)
        return top, total, jnp.dot(w, values, preferred_element_type=F32)

    ones = jnp.ones((TILE, BS), BF16)
    sums = jnp.dot(ones, k_ref[...], preferred_element_type=F32)
    pooled_ref[...] = (sums / math.sqrt(BS)).astype(BF16)
    own_max, own_total, own_sum = part(k_ref[...], v_ref[...])
    copies[0].wait()
    far_max, far_total, far_sum = part(far_ref[pl.ds(0, BS), :], far_ref[pl.ds(BS, BS), :])
    joint = jnp.maximum(own_max, far_max)
    own_e = jnp.exp2(own_max - joint)
    far_e = jnp.exp2(far_max - joint)
    inverse = 1.0 / (own_e * own_total + far_e * far_total)
    out_ref[...] = ((own_e * inverse) * own_sum + (far_e * inverse) * far_sum).astype(BF16)


def attend(me, d, q, packed):
    def rows(n):
        return pl.BlockSpec((BS, DH), lambda i, m: (n, 0))

    return pl.pallas_call(
        attend_kernel,
        grid_spec=pltpu.PrefetchScalarGridSpec(
            num_scalar_prefetch=1,
            grid=(1,),
            in_specs=[
                rows(0),
                pl.BlockSpec((TILE, DH), lambda i, m: (q.shape[0] // TILE - 1, 0)),
                rows(0),
                rows(1),
            ]
            + [pl.BlockSpec(memory_space=pl.ANY)] * len(packed),
            out_specs=[rows(0), pl.BlockSpec((TILE, DH), lambda i, m: (0, 0))],
            scratch_shapes=[pltpu.VMEM((2 * BS, DH), BF16), pltpu.SemaphoreType.DMA],
        ),
        out_shape=[
            jax.ShapeDtypeStruct((BS, DH), BF16),
            jax.ShapeDtypeStruct((TILE, DH), BF16),
        ],
        compiler_params=pltpu.CompilerParams(vmem_limit_bytes=16 << 20),
        cost_estimate=pl.CostEstimate(
            flops=8 * BS * BS * DH, transcendentals=2 * BS * BS, bytes_accessed=12 * BS * DH
        ),
    )(me, q, q, packed[d], packed[d], *packed)


def join_kernel(members, me_ref, *refs):
    pieces, out_ref = refs[:members], refs[members]
    for d in range(members):
        first = pl.multiple_of((me_ref[0] ^ d) * DH, DH)
        out_ref[:, pl.ds(first, DH)] = pieces[d][...]


def join_heads(me, pieces):
    members = len(pieces)
    tok = pieces[0].shape[0]
    piece = pl.BlockSpec((tok, DH), lambda i, m: (0, 0))
    return pl.pallas_call(
        functools.partial(join_kernel, members),
        grid_spec=pltpu.PrefetchScalarGridSpec(
            num_scalar_prefetch=1,
            grid=(1,),
            in_specs=[piece] * members,
            out_specs=pl.BlockSpec((tok, members * DH), lambda i, m: (0, 0)),
        ),
        out_shape=jax.ShapeDtypeStruct((tok, members * DH), BF16),
        compiler_params=pltpu.CompilerParams(vmem_limit_bytes=16 << 20),
        cost_estimate=pl.CostEstimate(
            flops=0, transcendentals=0, bytes_accessed=4 * members * tok * DH
        ),
    )(me, *pieces)


def after(x, *earlier):
    return lax.optimization_barrier((x, *earlier))[0]


def by_heads(query_rows, key_rows, value_rows, selection):
    members = lax.axis_size("context")
    me = lax.axis_index("context")
    tok, width = query_rows.shape
    heads = width // DH
    here = me.astype(jnp.int32)[None]
    near = list(range(1, members // 2))
    far = list(range(members // 2, members))[::-1]

    def send(x, d):
        return lax.ppermute(x, "context", [(i, i ^ d) for i in range(members)])

    packed = [pack_head(here, d, key_rows, value_rows) for d in range(members)]
    got = {}

    def exchange(pieces, kind, ds, window, done):
        for d in ds:
            earlier = [got[done[-window]]] if len(done) >= window else []
            got[kind, d] = send(after(pieces[d], *earlier), d)
            done.append((kind, d))

    far_done, near_done = [], []
    exchange(packed, 0, far[::-1], 3, far_done)
    exchange(packed, 0, near, 2, near_done)
    chosen = jnp.broadcast_to(selection.astype(BF16)[:, :, None], (heads, TILE, DH))
    pooled_q, *pieces = cut_queries(
        here, after(query_rows, got[0, members // 2], packed[0]), key_rows, chosen
    )
    exchange(pieces, 1, [2, 1, 3], 2, near_done)
    exchange(pieces, 1, far[::-1], 3, far_done)
    packed = packed[:1] + [got[0, d] for d in range(1, members)]
    queries = pieces[:1] + [got[1, d] for d in range(1, members)]
    outputs, rebuilt = [None] * members, [None] * members
    for d in [0] + far[::-1] + near:
        outputs[d], rebuilt[d] = attend(here, d, queries[d], packed)
        if d:
            outputs[d] = send(outputs[d], d)
    attended = join_heads(here, outputs)
    sort_logits = logits_of(here, pooled_q, queries, rebuilt)
    return attended, sort_logits.reshape(heads, 1, members)


def solution(mesh):
    members = mesh.shape["context"]

    def per_device(query_rows, key_rows, value_rows, selection):
        tok, width = query_rows.shape
        fits = tok == BS and width == members * DH and members & (members - 1) == 0
        if fits and members == TILE:
            return by_heads(query_rows, key_rows, value_rows, selection)
        return any_size(query_rows, key_rows, value_rows, selection)

    placed = (
        P(("groups", "context"), "tensor"),
        P(("groups", "context"), "tensor"),
        P(("groups", "context"), "tensor"),
        P("tensor", ("groups", "context")),
    )
    return jax.shard_map(
        per_device,
        mesh=mesh,
        in_specs=placed,
        out_specs=(P(("groups", "context"), "tensor"), P("tensor", ("groups", "context"), None)),
        check_vma=False,
    )
```

```python
import functools
import math

import jax
import jax.numpy as jnp
from jax import lax
from jax.experimental import pallas as pl
from jax.experimental.pallas import tpu as pltpu
from jax.sharding import PartitionSpec as P

DH = 128
BS = 512
BF16 = jnp.bfloat16
F32 = jnp.float32


def block_partial(query_block, key_block, value_block):
    scores = jnp.dot(query_block, key_block.T, preferred_element_type=jnp.float32) * (
        1.0 / math.sqrt(DH)
    )
    row_max = jnp.max(scores, axis=1, keepdims=True)
    weights = jnp.exp(scores - row_max).astype(jnp.bfloat16)
    row_total = jnp.sum(weights.astype(jnp.float32), axis=1, keepdims=True)
    partial_sum = jnp.dot(weights, value_block, preferred_element_type=jnp.float32)
    return (row_max, row_total, partial_sum)


def combine_parts(own_part, far_part):
    own_max, own_total, own_sum = own_part
    far_max, far_total, far_sum = far_part
    joint = jnp.maximum(own_max, far_max)
    own_factor = jnp.exp(own_max - joint)
    far_factor = jnp.exp(far_max - joint)
    merged = (own_factor * own_sum + far_factor * far_sum) / (
        own_factor * own_total + far_factor * far_total
    )
    return merged.astype(jnp.bfloat16)


def any_size(query_rows, key_rows, value_rows, selection):
    members = lax.axis_size("context")
    tok_rows, width = query_rows.shape
    blocks = tok_rows // BS
    head_count = width // DH
    piece_rows = BS // members

    def pooled(rows_in):
        sums = jnp.sum(rows_in.reshape(blocks, BS, width), axis=1, dtype=jnp.float32) / math.sqrt(
            BS
        )
        return sums.astype(jnp.bfloat16).reshape(blocks, head_count, DH).transpose(1, 0, 2)

    pooled_q = pooled(query_rows)
    pooled_k = pooled(key_rows)
    products = jnp.einsum(
        "hbd,hcd->hbc",
        pooled_q,
        lax.all_gather(pooled_k, "context", axis=1, tiled=True),
        preferred_element_type=jnp.float32,
    )
    sort_logits = products / math.sqrt(DH)
    wanted = lax.all_gather(selection, "context", axis=1, tiled=True)
    query_grid = query_rows.reshape(blocks, BS, head_count, DH)
    key_grid = key_rows.reshape(blocks, BS, head_count, DH)
    value_grid = value_rows.reshape(blocks, BS, head_count, DH)
    pair_ids = jnp.arange(blocks * head_count, dtype=jnp.int32)

    def slice_pair(array, block, head):
        return lax.dynamic_slice(array, (block, 0, head, 0), (1, BS, 1, DH)).reshape(BS, DH)

    def pick_rows(held, table):
        inner = held.shape[-1] // head_count
        order_ids = table.reshape(head_count, members, blocks).transpose(2, 1, 0)
        source_dev = (order_ids // blocks)[:, :, None, :]
        source_blk = (order_ids % blocks)[:, :, None, :]
        row_ids = jnp.arange(piece_rows)[None, None, :, None]
        head_ids = jnp.arange(head_count)[None, None, None, :]
        grid = held.reshape(blocks, members, piece_rows, head_count, inner)
        return grid[source_blk, source_dev, row_ids, head_ids].reshape(
            blocks, members, piece_rows, head_count * inner
        )

    spread_k = key_rows.reshape(blocks, members, piece_rows, width)
    spread_v = value_rows.reshape(blocks, members, piece_rows, width)
    held_k = lax.all_to_all(spread_k, "context", split_axis=1, concat_axis=1, tiled=True)
    held_v = lax.all_to_all(spread_v, "context", split_axis=1, concat_axis=1, tiled=True)
    far_k = lax.all_to_all(
        pick_rows(held_k, wanted), "context", split_axis=1, concat_axis=1, tiled=True
    )
    far_v = lax.all_to_all(
        pick_rows(held_v, wanted), "context", split_axis=1, concat_axis=1, tiled=True
    )
    far_keys = far_k.reshape(blocks, BS, head_count, DH)
    far_values = far_v.reshape(blocks, BS, head_count, DH)

    def both_pair(pair_index):
        block = pair_index // head_count
        head = pair_index % head_count
        query_block = slice_pair(query_grid, block, head)
        own = block_partial(
            query_block, slice_pair(key_grid, block, head), slice_pair(value_grid, block, head)
        )
        far = block_partial(
            query_block, slice_pair(far_keys, block, head), slice_pair(far_values, block, head)
        )
        return combine_parts(own, far)

    outputs = lax.map(both_pair, pair_ids)
    attended = (
        outputs.reshape(blocks, head_count, BS, DH).transpose(0, 2, 1, 3).reshape(tok_rows, width)
    )
    return (attended, sort_logits)


SCALE = math.log2(math.e) / math.sqrt(DH)
TILE = 8


def pack_kernel(me_ref, k_ref, v_ref, out_ref):
    out_ref[pl.ds(0, BS), :] = k_ref[...]
    out_ref[pl.ds(BS, BS), :] = v_ref[...]


def pack_head(me, d, k, v):
    rows = 2 * BS
    part = pl.BlockSpec((BS, DH), lambda i, m: (0, m[0] ^ d))
    return pl.pallas_call(
        pack_kernel,
        grid_spec=pltpu.PrefetchScalarGridSpec(
            num_scalar_prefetch=1,
            grid=(1,),
            in_specs=[part, part],
            out_specs=pl.BlockSpec((rows, DH), lambda i, m: (0, 0)),
        ),
        out_shape=jax.ShapeDtypeStruct((rows, DH), BF16),
        cost_estimate=pl.CostEstimate(
            flops=0, transcendentals=0, bytes_accessed=4 * rows * DH
        ),
    )(me, k, v)


def pooled(array):
    return (jnp.sum(array.astype(F32), axis=0, keepdims=True) / math.sqrt(BS)).astype(BF16)


def cut_kernel(heads, me_ref, q_ref, k_ref, chosen_ref, pooled_ref, *pieces):
    def by_head(row):
        return jnp.concatenate([row[:, h * DH : (h + 1) * DH] for h in range(heads)], axis=0)

    pooled_ref[...] = by_head(pooled(q_ref[...]))
    pooled_keys = by_head(pooled(k_ref[...]))
    for d in range(heads):
        first = pl.multiple_of((me_ref[0] ^ d) * DH, DH)
        pieces[d][pl.ds(0, BS), :] = q_ref[:, pl.ds(first, DH)]
        pieces[d][pl.ds(BS, heads), :] = pooled_keys
        pieces[d][pl.ds(BS + heads, TILE), :] = chosen_ref[me_ref[0] ^ d]


def cut_queries(me, q, k, chosen):
    tok, width = q.shape
    heads = width // DH
    whole = pl.BlockSpec((tok, width), lambda i, m: (0, 0))
    piece = pl.BlockSpec((tok + heads + TILE, DH), lambda i, m: (0, 0))
    return pl.pallas_call(
        functools.partial(cut_kernel, heads),
        grid_spec=pltpu.PrefetchScalarGridSpec(
            num_scalar_prefetch=1,
            grid=(1,),
            in_specs=[whole, whole, pl.BlockSpec((heads, TILE, DH), lambda i, m: (0, 0, 0))],
            out_specs=[pl.BlockSpec((heads, DH), lambda i, m: (0, 0))] + [piece] * heads,
        ),
        out_shape=[jax.ShapeDtypeStruct((heads, DH), BF16)]
        + [jax.ShapeDtypeStruct((tok + heads + TILE, DH), BF16)] * heads,
        compiler_params=pltpu.CompilerParams(vmem_limit_bytes=24 << 20),
        cost_estimate=pl.CostEstimate(
            flops=2 * tok * width, transcendentals=0, bytes_accessed=6 * tok * width
        ),
    )(me, q, k, chosen)


def logits_kernel(heads, me_ref, pooled_ref, *refs):
    pieces, out_ref = refs[:heads], refs[heads]
    q = pooled_ref[...].astype(F32)
    lane = lax.broadcasted_iota(jnp.int32, (heads, heads), 1)
    logits = jnp.zeros((heads, heads), F32)
    for d in range(heads):
        one = jnp.sum(q * pieces[d][...].astype(F32), axis=1, keepdims=True)
        logits = jnp.where(lane == (me_ref[0] ^ d), one / math.sqrt(DH), logits)
    out_ref[...] = logits


def logits_of(me, pooled_q, pieces):
    heads = len(pieces)
    rows = pl.BlockSpec((heads, DH), lambda i, m: (BS // heads, 0))
    return pl.pallas_call(
        functools.partial(logits_kernel, heads),
        grid_spec=pltpu.PrefetchScalarGridSpec(
            num_scalar_prefetch=1,
            grid=(1,),
            in_specs=[pl.BlockSpec((heads, DH), lambda i, m: (0, 0))] + [rows] * heads,
            out_specs=pl.BlockSpec((heads, heads), lambda i, m: (0, 0)),
        ),
        out_shape=jax.ShapeDtypeStruct((heads, heads), F32),
    )(me, pooled_q, *pieces)


def attend_kernel(me_ref, q_ref, tile_ref, k_ref, v_ref, *refs):
    packed, (out_ref, far_ref, sem) = refs[:-3], refs[-3:]
    source = me_ref[0] ^ jnp.max(tile_ref[...].astype(F32)).astype(jnp.int32)
    copies = [pltpu.make_async_copy(one, far_ref, sem) for one in packed]
    for n, copy in enumerate(copies):
        pl.when(source == n)(copy.start)
    q = q_ref[...]

    def part(keys, values):
        s = lax.dot_general(q, keys, (((1,), (1,)), ((), ())), preferred_element_type=F32)
        top = jnp.max(s, axis=1, keepdims=True) * SCALE
        w = jnp.exp2(s * SCALE - top).astype(BF16)
        total = jnp.sum(w.astype(F32), axis=1, keepdims=True)
        return top, total, jnp.dot(w, values, preferred_element_type=F32)

    own_max, own_total, own_sum = part(k_ref[...], v_ref[...])
    copies[0].wait()
    far_max, far_total, far_sum = part(far_ref[pl.ds(0, BS), :], far_ref[pl.ds(BS, BS), :])
    joint = jnp.maximum(own_max, far_max)
    own_e = jnp.exp2(own_max - joint)
    far_e = jnp.exp2(far_max - joint)
    inverse = 1.0 / (own_e * own_total + far_e * far_total)
    out_ref[...] = ((own_e * inverse) * own_sum + (far_e * inverse) * far_sum).astype(BF16)


def attend(me, d, q, packed):
    def rows(n):
        return pl.BlockSpec((BS, DH), lambda i, m: (n, 0))

    return pl.pallas_call(
        attend_kernel,
        grid_spec=pltpu.PrefetchScalarGridSpec(
            num_scalar_prefetch=1,
            grid=(1,),
            in_specs=[
                rows(0),
                pl.BlockSpec((TILE, DH), lambda i, m: (q.shape[0] // TILE - 1, 0)),
                rows(0),
                rows(1),
            ]
            + [pl.BlockSpec(memory_space=pl.ANY)] * len(packed),
            out_specs=rows(0),
            scratch_shapes=[pltpu.VMEM((2 * BS, DH), BF16), pltpu.SemaphoreType.DMA],
        ),
        out_shape=jax.ShapeDtypeStruct((BS, DH), BF16),
        compiler_params=pltpu.CompilerParams(vmem_limit_bytes=16 << 20),
        cost_estimate=pl.CostEstimate(
            flops=8 * BS * BS * DH, transcendentals=2 * BS * BS, bytes_accessed=12 * BS * DH
        ),
    )(me, q, q, packed[d], packed[d], *packed)


def join_kernel(members, me_ref, *refs):
    pieces, out_ref = refs[:members], refs[members]
    for d in range(members):
        first = pl.multiple_of((me_ref[0] ^ d) * DH, DH)
        out_ref[:, pl.ds(first, DH)] = pieces[d][...]


def join_heads(me, pieces):
    members = len(pieces)
    tok = pieces[0].shape[0]
    piece = pl.BlockSpec((tok, DH), lambda i, m: (0, 0))
    return pl.pallas_call(
        functools.partial(join_kernel, members),
        grid_spec=pltpu.PrefetchScalarGridSpec(
            num_scalar_prefetch=1,
            grid=(1,),
            in_specs=[piece] * members,
            out_specs=pl.BlockSpec((tok, members * DH), lambda i, m: (0, 0)),
        ),
        out_shape=jax.ShapeDtypeStruct((tok, members * DH), BF16),
        compiler_params=pltpu.CompilerParams(vmem_limit_bytes=16 << 20),
        cost_estimate=pl.CostEstimate(
            flops=0, transcendentals=0, bytes_accessed=4 * members * tok * DH
        ),
    )(me, *pieces)


def after(x, *earlier):
    return lax.optimization_barrier((x, *earlier))[0]


def by_heads(query_rows, key_rows, value_rows, selection):
    members = lax.axis_size("context")
    me = lax.axis_index("context")
    tok, width = query_rows.shape
    heads = width // DH
    here = me.astype(jnp.int32)[None]
    near = list(range(1, members // 2))
    far = list(range(members // 2, members))[::-1]

    def send(x, d):
        return lax.ppermute(x, "context", [(i, i ^ d) for i in range(members)])

    packed = [pack_head(here, d, key_rows, value_rows) for d in range(members)]
    column = (me ^ (members // 2)) * DH
    packed[members // 2] = jnp.concatenate(
        [lax.dynamic_slice_in_dim(x, column, DH, axis=1) for x in (key_rows, value_rows)]
    )
    got = {}

    def exchange(pieces, kind, ds, window, done):
        for d in ds:
            earlier = [got[done[-window]]] if len(done) >= window else []
            got[kind, d] = send(after(pieces[d], *earlier), d)
            done.append((kind, d))

    far_done, near_done = [], []
    exchange(packed, 0, far[::-1], 3, far_done)
    exchange(packed, 0, near, 2, near_done)
    chosen = jnp.broadcast_to(selection.astype(BF16)[:, :, None], (heads, TILE, DH))
    pooled_q, *pieces = cut_queries(
        here, after(query_rows, got[0, members // 2], packed[0]), key_rows, chosen
    )
    exchange(pieces, 1, [2, 1, 3], 2, near_done)
    exchange(pieces, 1, far[::-1], 3, far_done)
    packed = packed[:1] + [got[0, d] for d in range(1, members)]
    queries = pieces[:1] + [got[1, d] for d in range(1, members)]
    sort_logits = logits_of(here, pooled_q, queries)

    outputs = [None] * members
    for d in [0] + far[::-1] + near:
        outputs[d] = attend(here, d, queries[d], packed)
        if d:
            outputs[d] = send(outputs[d], d)
    attended = join_heads(here, outputs)
    return attended, sort_logits.reshape(heads, 1, members)


def solution(mesh):
    members = mesh.shape["context"]

    def per_device(query_rows, key_rows, value_rows, selection):
        tok, width = query_rows.shape
        fits = tok == BS and width == members * DH and members & (members - 1) == 0
        if fits and members == TILE:
            return by_heads(query_rows, key_rows, value_rows, selection)
        return any_size(query_rows, key_rows, value_rows, selection)

    placed = (
        P(("groups", "context"), "tensor"),
        P(("groups", "context"), "tensor"),
        P(("groups", "context"), "tensor"),
        P("tensor", ("groups", "context")),
    )
    return jax.shard_map(
        per_device,
        mesh=mesh,
        in_specs=placed,
        out_specs=(P(("groups", "context"), "tensor"), P("tensor", ("groups", "context"), None)),
        check_vma=False,
    )
```
